32 devices in a mesh: seq: 8 (over z, core), head: 4 (over y, x).
Axes of the slice: x: 2, y: 2, z: 4, core: 2. Of those that a mesh axis runs over, the one named last changes fastest.
Arguments:
- attn_query: bfloat16 [16384, 2560], P('seq', 'head'), may hold values from -45 to 45
- attn_key: bfloat16 [16384, 2560], P('seq', 'head'), may hold values from -15 to 15
- attn_value: bfloat16 [16384, 2560], P('seq', 'head'), may hold values from -6 to 6
- fast_query: bfloat16 [16384, 2560], P('seq', 'head'), may hold values from -6 to 6
- fast_key: bfloat16 [16384, 2560], P('seq', 'head'), may hold values from -6 to 6
- fast_value: bfloat16 [16384, 2560], P('seq', 'head'), may hold values from -6 to 6
- rates: float32 [16384, 4], P('seq', 'head'), may hold values from 0.00022097086 to 0.0022097088
- fast_weights: float32 [4, 640, 3, 640], P('head'), may hold values from -0.25 to 0.25
- gain: float32 [4, 640], P('head'), may hold values from 0.5 to 1.5
Outputs:
- mixed: bfloat16 [16384, 2560], P('seq', 'head')
- final_weights: float32 [4, 640, 3, 640], P('head', 'seq')
The draws below stay inside these ranges and needn't reach their ends.
All inputs are finite; a program needn't handle non-finite values.
Results may differ from the reference program's by a relative error of at most 0.013.
Values may be sent and summed in bfloat16 or wider, within the bound.
A program may use at most 192 MiB of HBM per device.

```python
import math
import jax
import jax.numpy as jnp
from jax import lax

DH = 640
FH = 640
AH = 128
WINDOW = 512
HEADS = 4
ATT_HEADS = 20
TOKENS = 16384


def attention_pair(seed_key):
    grid_shape = (TOKENS, ATT_HEADS * AH)
    base_key = jnp.clip(jax.random.normal(jax.random.fold_in(seed_key, 101), grid_shape, jnp.float32), -5.0, 5.0)
    base_query = jnp.clip(jax.random.normal(jax.random.fold_in(seed_key, 202), grid_shape, jnp.float32), -5.0, 5.0)
    return (base_query, base_key)


def draw_attn_query(key, part):
    return attention_pair(key)[0].astype(jnp.bfloat16)


def draw_attn_key(key, part):
    return attention_pair(key)[1].astype(jnp.bfloat16)


def level_of(key, dims, split, smallest, high):
    def one(axis_at, parts):
        steps = jax.random.uniform(jax.random.fold_in(jax.random.fold_in(key, 6), axis_at), (parts,), jnp.float32, smallest / len(split), high / len(split))
        return jnp.repeat(jnp.exp(steps), dims[axis_at] // parts).reshape((-1,) + (1,) * (len(dims) - axis_at - 1))

    level = one(*split[0])
    for cut in split[1:]:
        level = level * one(*cut)
    return level


def normal_values(own_key, dims, scale, reach, cuts=(), held_as=jnp.bfloat16):
    drawn = jax.random.normal(own_key, dims, jnp.float32) * scale
    if len(cuts) > 0:
        drawn = level_of(own_key, dims, cuts, -0.22, 0.18) * drawn
    return jnp.clip(drawn, min=-reach, max=reach).astype(held_as)


def setup_inputs(seed: int = 0) -> dict:
    arg_keys = jax.random.split(jax.random.key(seed), 10)
    attn_query = draw_attn_query(jax.random.fold_in(arg_keys[9], 71), 0)
    attn_key = draw_attn_key(jax.random.fold_in(arg_keys[9], 71), 0)
    attn_value = normal_values(arg_keys[2], (TOKENS, ATT_HEADS * AH), 1.0, 6.0, ((0, 8), (1, 4)))
    fast_query = normal_values(arg_keys[3], (TOKENS, HEADS * DH), 1.0, 6.0, ((0, 8), (1, 4)))
    fast_key = normal_values(arg_keys[4], (TOKENS, HEADS * DH), 1.0, 6.0, ((0, 8), (1, 4)))
    fast_value = normal_values(arg_keys[5], (TOKENS, HEADS * DH), 1.0, 6.0, ((0, 8), (1, 4)))
    rates = jnp.clip(jnp.exp(math.log(0.0022097088) - 2.3025852 * jax.random.uniform(arg_keys[6], (TOKENS, HEADS), jnp.float32) ** level_of(arg_keys[6], (TOKENS, HEADS), ((0, 8), (1, 4)), -0.2, 0.2)), 0.00022097086, 0.0022097088)
    fast_weights = normal_values(arg_keys[7], (HEADS, FH, 3, DH), DH ** -0.5, 0.25, ((0, 4),), jnp.float32)
    gain = jnp.clip(1.0 + 0.1 * jax.random.normal(arg_keys[8], (HEADS, DH), jnp.float32), 0.5, 1.5)
    return dict(attn_query=attn_query, attn_key=attn_key, attn_value=attn_value, fast_query=fast_query, fast_key=fast_key, fast_value=fast_value, rates=rates, fast_weights=fast_weights, gain=gain)


EPSILON = 1e-06

def window_attention(queries, key_rows, value_rows):
    total_rows, columns = queries.shape
    head_count = columns // AH
    tile_rows = min(total_rows, 512)
    zero_rows = jnp.zeros((WINDOW, columns), queries.dtype)
    padded_keys = jnp.concatenate([zero_rows, key_rows], 0)
    padded_values = jnp.concatenate([zero_rows, value_rows], 0)

    def one_tile(tile_index):
        tile_start = tile_index * tile_rows
        query_tile = lax.dynamic_slice_in_dim(queries, tile_start, tile_rows, 0).astype(jnp.float32).reshape(tile_rows, head_count, AH)
        key_tile = lax.dynamic_slice_in_dim(padded_keys, tile_start, tile_rows + WINDOW, 0).astype(jnp.float32).reshape(tile_rows + WINDOW, head_count, AH)
        value_tile = lax.dynamic_slice_in_dim(padded_values, tile_start, tile_rows + WINDOW, 0).astype(jnp.float32).reshape(tile_rows + WINDOW, head_count, AH)
        scores = jnp.einsum('qhd,khd->hqk', query_tile, key_tile) * (1.0 / math.sqrt(AH))
        query_pos = tile_start + jnp.arange(tile_rows, dtype=jnp.int32)
        key_pos = tile_start - WINDOW + jnp.arange(tile_rows + WINDOW, dtype=jnp.int32)
        distance = query_pos[:, None] - key_pos[None, :]
        allowed = (distance >= 0) & (distance < WINDOW) & (key_pos[None, :] >= 0)
        scores = jnp.where(allowed[None], scores, -1e+30)
        row_max = lax.optimization_barrier(jnp.max(scores, axis=-1, keepdims=True))
        weights = jnp.exp(scores - row_max)
        row_total = lax.optimization_barrier(jnp.sum(weights, axis=-1, keepdims=True))
        probabilities = (weights / row_total).astype(jnp.bfloat16)
        result = jnp.einsum('hqk,khd->qhd', probabilities.astype(jnp.float32), value_tile)
        return result.reshape(tile_rows, columns)
    tiles = lax.map(one_tile, jnp.arange(total_rows // tile_rows, dtype=jnp.int32))
    return tiles.reshape(total_rows, columns)

def block_gradient(weights, key_rows, value_rows, rate_rows):
    gate_pre = jnp.dot(key_rows, weights[:, 0, :].T, preferred_element_type=jnp.float32)
    up_pre = jnp.dot(key_rows, weights[:, 1, :].T, preferred_element_type=jnp.float32)
    active = jax.nn.silu(gate_pre)
    hidden = (active * up_pre).astype(jnp.bfloat16)
    signal = (rate_rows * value_rows.astype(jnp.float32)).astype(jnp.bfloat16)
    back_grad = jnp.dot(signal, weights[:, 2, :].T, preferred_element_type=jnp.float32)
    sigmoid_gate = jax.nn.sigmoid(gate_pre)
    up_grad = (back_grad * active).astype(jnp.bfloat16)
    gate_grad = (back_grad * up_pre * sigmoid_gate * (1.0 + gate_pre * (1.0 - sigmoid_gate))).astype(jnp.bfloat16)
    gate_term = jnp.dot(gate_grad.T, key_rows, preferred_element_type=jnp.float32)
    up_term = jnp.dot(up_grad.T, key_rows, preferred_element_type=jnp.float32)
    down_term = jnp.dot(hidden.T, signal, preferred_element_type=jnp.float32)
    return jnp.stack([gate_term, up_term, down_term], axis=1)

def renormalize(previous, gradient):
    moved = previous + gradient
    norm_ratio = jnp.sqrt(lax.optimization_barrier(jnp.mean(previous * previous, axis=-1, keepdims=True)) + EPSILON) / jnp.sqrt(lax.optimization_barrier(jnp.mean(moved * moved, axis=-1, keepdims=True)) + EPSILON)
    return moved * norm_ratio

def fast_apply(weights, query_rows, gain_row):
    gate_pre = jnp.dot(query_rows, weights[:, 0, :].T, preferred_element_type=jnp.float32)
    up_pre = jnp.dot(query_rows, weights[:, 1, :].T, preferred_element_type=jnp.float32)
    hidden = (jax.nn.silu(gate_pre) * up_pre).astype(jnp.bfloat16)
    output = jnp.dot(hidden, weights[:, 2, :], preferred_element_type=jnp.float32)
    inverse_rms = lax.rsqrt(lax.optimization_barrier(jnp.mean(output * output, axis=-1, keepdims=True)) + EPSILON)
    return output * inverse_rms * gain_row

def reference(attn_query, attn_key, attn_value, fast_query, fast_key, fast_value, rates, fast_weights, gain):
    attended = window_attention(attn_query, attn_key, attn_value)
    half_rows = TOKENS // 2
    pieces = []
    finals = []
    for head_index in range(HEADS):
        low = head_index * DH
        head_queries = fast_query[:, low:low + DH]
        head_keys = fast_key[:, low:low + DH]
        head_values = fast_value[:, low:low + DH]
        head_rates = rates[:, head_index:head_index + 1]
        initial = fast_weights[head_index]
        first_cast = initial.astype(jnp.bfloat16)
        first_gradient = block_gradient(first_cast, head_keys[:half_rows], head_values[:half_rows], head_rates[:half_rows])
        middle = renormalize(initial, first_gradient)
        middle_cast = middle.astype(jnp.bfloat16)
        second_gradient = block_gradient(middle_cast, head_keys[half_rows:], head_values[half_rows:], head_rates[half_rows:])
        finals.append(renormalize(middle, second_gradient))
        early_out = fast_apply(first_cast, head_queries[:half_rows], gain[head_index])
        later_out = fast_apply(middle_cast, head_queries[half_rows:], gain[head_index])
        pieces.append(jnp.concatenate([early_out, later_out], 0))
    mixed = (attended + jnp.concatenate(pieces, 1)).astype(jnp.bfloat16)
    return (mixed, jnp.stack(finals))
```

```python
import functools
import math
from types import SimpleNamespace

import jax
import jax.numpy as jnp
from jax import lax
from jax.experimental import pallas as pl
from jax.experimental.pallas import tpu as pltpu
from jax.sharding import PartitionSpec as P

AH = 128
WINDOW = 512
EPSILON = 1e-06
NEG = -1e30
NT = (((1,), (1,)), ((), ()))
NN = (((1,), (0,)), ((), ()))
LIMIT = 62 * 1024 * 1024
UNIT = 32
PACK = 2
TILE = 1024
BF = jnp.bfloat16
F32 = jnp.float32


def mm(a, b, dims):
    return lax.dot_general(a, b, dims, preferred_element_type=jnp.float32)


def sigmoid(v):
    return 0.5 * jnp.tanh(0.5 * v) + 0.5


def attend(q, keys, values, biases):
    rows = q.shape[0]
    factor = math.log2(math.e) / math.sqrt(AH)
    old, mid, new = (mm(q, k, NT) for k in keys)
    if biases[0] is not None:
        old = old + biases[0]
    if biases[1] is not None:
        mid = mid + biases[1]
    row = lax.broadcasted_iota(jnp.int32, (rows, rows), 0)
    col = lax.broadcasted_iota(jnp.int32, (rows, rows), 1)
    causal = col <= row
    edge = jnp.where(causal, new, old)
    top = jnp.maximum(jnp.max(edge, -1, keepdims=True), jnp.max(mid, -1, keepdims=True))
    edge = jnp.exp2((edge - top) * factor)
    mid = jnp.exp2((mid - top) * factor)
    total = jnp.sum(edge, -1, keepdims=True) + jnp.sum(mid, -1, keepdims=True)
    p_new = jnp.where(causal, edge, 0.0).astype(BF)
    p_old = jnp.where(causal, 0.0, edge).astype(BF)
    out = mm(p_new, values[2], NN) + mm(p_old, values[0], NN)
    out = out + mm(mid.astype(BF), values[1], NN)
    return out * (1.0 / total)


def renormalize(previous, grad):
    moved = previous + grad
    return moved * (
        jnp.sqrt(jnp.mean(previous * previous, axis=-1, keepdims=True) + EPSILON)
        / jnp.sqrt(jnp.mean(moved * moved, axis=-1, keepdims=True) + EPSILON)
    )


def sizes(count, rows, d, f, columns):
    half = count // 2
    chips = half // 2
    rpo = UNIT // chips
    share = f // count
    per_block = share // rpo
    groups = 2 * per_block
    z = SimpleNamespace(
        count=count, half=half, chips=chips, rpo=rpo, share=share, nb=per_block, ng=groups,
        ns=groups // PACK, rows=rows, d=d, heads=columns // AH,
    )
    assert z.rpo * z.chips == UNIT and z.nb * z.rpo == z.share and z.ns * PACK == z.ng
    assert z.heads == z.ns and z.ns >= 3 + (z.nb - 1) // PACK
    return z


def scratch(z):
    unit = (3, UNIT, z.d)
    piece = (3, z.rpo, z.d)
    tokens = pltpu.VMEM((z.rows, z.d), BF)
    halo = pltpu.VMEM((WINDOW, z.d), BF)
    dma = pltpu.SemaphoreType.DMA
    return dict(
        qs=tokens, ks=tokens, vs=tokens, fqs=tokens, xs=tokens, ys=tokens, outs=tokens,
        att=pltpu.VMEM((z.rows, z.d), F32),
        app=pltpu.VMEM((z.rows, z.d), F32),
        hk=halo, hv=halo,
        wf=pltpu.VMEM((z.ng, 2, 3, z.chips, z.rpo, z.d), F32),
        wb=pltpu.VMEM((z.ng, 2) + unit, BF),
        acc=pltpu.VMEM((PACK, 2) + unit, F32),
        gsum=pltpu.VMEM((z.ng,) + unit, F32),
        pair_s=pltpu.VMEM((z.ng,) + unit, BF),
        pair_r=pltpu.VMEM((z.ng,) + unit, BF),
        chain_s=pltpu.VMEM((z.ng,) + unit, BF),
        chain_r=pltpu.VMEM((z.ng,) + unit, BF),
        midb=pltpu.VMEM((z.ng,) + unit, BF),
        midq=pltpu.VMEM((z.nb, z.chips) + piece, BF),
        ownm=pltpu.VMEM((z.nb,) + piece, BF),
        og_s=pltpu.VMEM((z.nb, z.chips) + piece, BF),
        ox_s=pltpu.VMEM((z.nb, z.chips) + piece, BF),
        og_r=pltpu.VMEM((z.nb,) + piece, BF),
        ox_r=pltpu.VMEM((z.nb, z.chips) + piece, BF),
        load_sem=dma((6,)), wf_sem=dma((z.ng, 2)), store_sem=dma((z.rows // 256,)),
        halo_ss=dma((2,)), halo_rs=dma((2,)),
        pair_ss=dma((z.ng,)), pair_rs=dma((z.ng,)),
        chain_ss=dma((z.ng,)), chain_rs=dma((z.ng,)),
        mid_ss=dma((z.ng,)), mid_rs=dma((z.ng,)),
        part_ss=dma((z.ng,)), part_rs=dma((z.ng,)),
        om_ss=dma((z.nb, z.chips)), om_rs=dma((z.nb,)),
        og_ss=dma((z.nb, z.chips)), og_rs=dma((z.nb,)),
        ox_ss=dma((z.nb, z.chips)), ox_rs=dma((z.nb, z.chips)),
    )


INPUTS = ("q", "k", "v", "fq", "fk", "fv", "rate", "w", "gain")


def kernel(z, names, *refs):
    r = SimpleNamespace(**dict(zip(names, refs)))
    s = lax.axis_index("seq")
    hd = lax.axis_index("head")
    chip = lax.div(s, 2)
    c = s - 2 * chip
    b = lax.div(chip, z.chips)
    p = chip - b * z.chips
    first, second = b == 0, b == 1
    head_chip, tail_chip = p == 0, p == z.chips - 1

    def both(*conditions):
        return functools.reduce(jnp.logical_and, conditions)

    def either(*conditions):
        return functools.reduce(jnp.logical_or, conditions)

    def remote(src, dst, ss, rs, device):
        return pltpu.make_async_remote_copy(
            src_ref=src, dst_ref=dst, send_sem=ss, recv_sem=rs,
            device_id=(device, hd), device_id_type=pl.DeviceIdType.MESH,
        )

    def pair(g):
        return remote(r.pair_s.at[g], r.pair_r.at[g], r.pair_ss.at[g], r.pair_rs.at[g], s + 1 - 2 * c)

    def chain(g):
        return remote(r.chain_s.at[g], r.chain_r.at[g], r.chain_ss.at[g], r.chain_rs.at[g], s + 2 - 4 * b)

    def mid_out(g):
        return remote(r.midb.at[g], r.wb.at[g, c], r.mid_ss.at[g], r.mid_rs.at[g], s + 2)

    def mid_on(g):
        return remote(r.wb.at[g, c], r.wb.at[g, c], r.mid_ss.at[g], r.mid_rs.at[g], s + 2)

    def mid_part(g, core):
        return remote(r.wb.at[g, core], r.wb.at[g, core], r.part_ss.at[g], r.part_rs.at[g], s + 1 - 2 * c)

    def own_mid(g, t):
        return remote(r.midq.at[g, t], r.ownm.at[g], r.om_ss.at[g, t], r.om_rs.at[g], 2 * t + c)

    def own_grad(g, t):
        return remote(r.og_s.at[g, t], r.og_r.at[g], r.og_ss.at[g, t], r.og_rs.at[g], 2 * t + c)

    def cross_grad(g, t, origin):
        return remote(
            r.ox_s.at[g, t], r.ox_r.at[g, origin], r.ox_ss.at[g, t], r.ox_rs.at[g, origin],
            z.half + 2 * t + c,
        )

    def halo(n):
        src, dst = ((r.k, r.hk), (r.v, r.hv))[n]
        return remote(
            src.at[pl.ds(z.rows - WINDOW, WINDOW)], dst, r.halo_ss.at[n], r.halo_rs.at[n], s + 1
        )

    def load(n):
        src, dst = (
            (r.q, r.qs), (r.k, r.ks), (r.v, r.vs), (r.fq, r.fqs), (r.fk, r.xs), (r.fv, r.ys)
        )[n]
        return pltpu.make_async_copy(src, dst, r.load_sem.at[n])

    def load_w(g, core):
        block = lax.div(g, z.nb)
        return pltpu.make_async_copy(
            r.w.at[:, block, :, core, g - block * z.nb], r.wf.at[g, core], r.wf_sem.at[g, core]
        )

    def peer(n):
        other, core, block = n // 2, n % 2, n // z.half
        near = b == block
        if other < z.chips:
            near = either(near, chip == z.chips)
        if other == z.chips:
            near = either(near, first)
        return both(s != n, either(both(c == core, near), s == n - 1, s == n + 1))

    barrier = pltpu.get_barrier_semaphore()
    for n in range(z.count):
        @pl.when(peer(n))
        def _():
            pl.semaphore_signal(
                barrier, inc=1, device_id=(n, hd), device_id_type=pl.DeviceIdType.MESH
            )

    @pl.when(first)
    def _():
        load(4).start()
        load(5).start()

        @pl.loop(0, z.ng)
        def _(g):
            for core in range(2):
                load_w(g, core).start()

    @pl.when(second)
    def _():
        for n in (0, 1, 2):
            load(n).start()

    @pl.when(s == 0)
    def _():
        r.hk[...] = jnp.zeros_like(r.hk)
        r.hv[...] = jnp.zeros_like(r.hv)

    pl.semaphore_wait(barrier, sum(jnp.where(peer(n), 1, 0) for n in range(z.count)))

    slow_halo = both(first, c == 1, p < z.chips - 1)

    @pl.when(s < z.count - 1)
    def _():
        halo(0).start()

        @pl.when(jnp.logical_not(slow_halo))
        def _():
            halo(1).start()

    @pl.when(first)
    def _():
        for n in (0, 1, 2, 3):
            load(n).start()

    @pl.when(second)
    def _():
        for n in (4, 5, 3):
            load(n).start()

    r.app[...] = jnp.zeros_like(r.app)

    def weights(i):
        w = r.wb[pl.ds(i * PACK, PACK)].reshape(PACK * 2, 3, UNIT, z.d)
        return w

    def grad_step(i):
        n = PACK * 2
        w = weights(i)
        w_gu = w[:, 0:2].reshape(n * 2 * UNIT, z.d)
        w_down = w[:, 2].reshape(n * UNIT, z.d)
        for t in range(z.rows // TILE):
            at = pl.ds(t * TILE, TILE)
            x, y, rate = r.xs[at, :], r.ys[at, :], r.rate[:, at]
            gu = mm(w_gu, x, NT).reshape(n, 2, UNIT, TILE)
            back = mm(w_down, y, NT) * rate
            gate = gu[:, 0].reshape(n * UNIT, TILE)
            up = gu[:, 1].reshape(n * UNIT, TILE)
            sg = sigmoid(gate)
            active = gate * sg
            hidden = (active * up * rate).astype(BF)
            up_grad = (back * active).astype(BF)
            gate_grad = (back * up * (sg * (1.0 + gate * (1.0 - sg)))).astype(BF)
            both_grad = jnp.concatenate(
                [gate_grad.reshape(n, 1, UNIT, TILE), up_grad.reshape(n, 1, UNIT, TILE)], 1
            ).reshape(n * 2 * UNIT, TILE)
            wide = mm(both_grad, x, NN).reshape(PACK, 2, 2, UNIT, z.d)
            down = mm(hidden, y, NN).reshape(PACK, 2, UNIT, z.d)
            if t == 0:
                r.acc[:, :, 0:2] = wide
                r.acc[:, :, 2] = down
            else:
                r.acc[:, :, 0:2] += wide
                r.acc[:, :, 2] += down
        for k in range(PACK):
            g = i * PACK + k
            r.gsum[g] = r.acc[k, c]
            r.pair_s[g] = r.acc[k, 1 - c].astype(BF)
            pair(g).start()

    def combine(g):
        pair(g).wait_recv()
        r.gsum[g] += r.pair_r[g].astype(F32)

    def add_chain(g):
        chain(g).wait_recv()
        r.gsum[g] += r.chain_r[g].astype(F32)

    def send_chain(g):
        r.chain_s[g] = r.gsum[g].astype(BF)
        chain(g).start()

    def split(unit):
        return unit.reshape(3, z.chips, z.rpo, z.d)

    def reduce_first(i):
        for k in range(PACK):
            g = i * PACK + k
            combine(g)

            @pl.when(p > 0)
            def _():
                add_chain(g)

            send_chain(g)

    def make_middle(i):
        for k in range(PACK):
            g = i * PACK + k
            combine(g)
            add_chain(g)
            middle = renormalize(r.wf[g, c].reshape(3, UNIT, z.d), r.gsum[g])
            r.midb[g] = middle.astype(BF)
            mid_out(g).start()

            @pl.when(g < z.nb)
            def _():
                pieces = split(middle)
                for t in range(z.chips):
                    r.midq[g, t] = pieces[:, t].astype(BF)
                    if t < z.chips - 1:
                        own_mid(g, t).start()

    def relay(i):
        for k in range(PACK):
            g = i * PACK + k
            mid_on(g).wait_recv()

            @pl.when(p < z.chips - 1)
            def _():
                mid_on(g).start()

            mid_part(g, c).start()
        for k in range(PACK):
            mid_part(i * PACK + k, 1 - c).wait_recv()

    def reduce_second(i):
        for k in range(PACK):
            g = i * PACK + k
            combine(g)

            @pl.when(both(g < z.nb, tail_chip))
            def _():
                send_chain(g)

            @pl.when(g >= z.nb)
            def _():
                pieces = split(r.gsum[g])
                for t in range(z.chips):
                    @pl.when(p != t)
                    def _():
                        r.ox_s[g - z.nb, t] = pieces[:, t].astype(BF)
                        cross_grad(g - z.nb, t, p).start()

    def hand_back(i):
        for k in range(PACK):
            g = i * PACK + k

            @pl.when(g < z.nb)
            def _():
                add_chain(g)

                @pl.when(p > 0)
                def _():
                    send_chain(g)

                @pl.when(head_chip)
                def _():
                    pieces = split(r.gsum[g])
                    for t in range(z.chips):
                        r.og_s[g, t] = pieces[:, t].astype(BF)
                        own_grad(g, t).start()

    tile = WINDOW // 2

    def attention_tile(h, t, bias):
        columns = pl.ds(pl.multiple_of(h * AH, AH), AH)

        def block(ref, halo_ref, at):
            if at < 0:
                return halo_ref[(at + 2) * tile : (at + 3) * tile, columns]
            return ref[at * tile : (at + 1) * tile, columns]

        keys = [block(r.ks, r.hk, t - 2 + n) for n in range(3)]
        values = [block(r.vs, r.hv, t - 2 + n) for n in range(3)]
        biases = [bias if t - 2 + n < 0 else None for n in range(2)]
        r.att[t * tile : (t + 1) * tile, columns] = attend(
            r.qs[t * tile : (t + 1) * tile, columns], keys, values, biases
        )

    def apply_step(i):
        n = PACK * 2
        w = weights(i)
        w_gate, w_up, w_down = (w[:, m].reshape(n * UNIT, z.d) for m in range(3))
        w_gu = jnp.concatenate([w_gate, w_up], 0)
        for t in range(z.rows // TILE):
            at = pl.ds(t * TILE, TILE)
            gu = mm(r.fqs[at, :], w_gu, NT)
            gate, up = gu[:, : n * UNIT], gu[:, n * UNIT :]
            hidden = (gate * sigmoid(gate) * up).astype(BF)
            r.app[at, :] += mm(hidden, w_down, NN)

    @pl.loop(0, 2 * z.ns)
    def _(j):
        early = j < z.ns
        i = lax.rem(j, z.ns)

        @pl.when(both(second, j >= z.ns))
        def _():
            relay(i)

        @pl.when(either(both(first, j == 0), both(second, j == z.ns)))
        def _():
            load(4).wait()
            load(5).wait()

        @pl.when(either(both(second, j == 0), both(first, j == z.ns)))
        def _():
            for n in (0, 1, 2):
                load(n).wait()

        @pl.when(j == z.ns)
        def _():
            load(3).wait()

        @pl.when(both(first, early))
        def _():
            for k in range(PACK):
                g = i * PACK + k
                for core in range(2):
                    load_w(g, core).wait()
                    r.wb[g, core] = r.wf[g, core].reshape(3, UNIT, z.d).astype(BF)

        differentiate = first == early

        @pl.when(differentiate)
        def _():
            grad_step(i)

        @pl.when(both(first, p < z.chips - 1, j >= 1, j <= z.ns))
        def _():
            reduce_first(j - 1)

        @pl.when(both(slow_halo, j == z.ns + 2))
        def _():
            halo(1).start()

        @pl.when(jnp.logical_not(differentiate))
        def _():
            for t in range(2, z.rows // tile):
                attention_tile(i, t, None)

        @pl.when(j >= z.ns)
        def _():
            apply_step(i)

        @pl.when(both(first, tail_chip, j >= 3, j < 3 + z.ns))
        def _():
            make_middle(j - 3)

        @pl.when(either(both(second, j == z.ns - 1), both(first, j == 2 * z.ns - 1)))
        def _():
            @pl.when(s > 0)
            def _():
                halo(0).wait_recv()
                halo(1).wait_recv()

            bias = jnp.where(s == 0, jnp.float32(NEG), jnp.float32(0.0))

            @pl.loop(0, z.heads)
            def _(h):
                for t in range(2):
                    attention_tile(h, t, bias)

        @pl.when(both(second, j >= z.ns))
        def _():
            reduce_second(i)

        @pl.when(both(second, p < z.chips - 1, j >= z.ns + 2))
        def _():
            hand_back(j - z.ns - 2)

    def store(t):
        at = pl.ds(t * 256, 256)
        return pltpu.make_async_copy(r.outs.at[at], r.mixed.at[at], r.store_sem.at[t])

    @pl.loop(0, z.rows // 256)
    def _(t):
        at = pl.ds(t * 256, 256)
        out = r.app[at, :]
        inverse = lax.rsqrt(jnp.mean(out * out, axis=-1, keepdims=True) + EPSILON)
        r.outs[at, :] = (r.att[at, :] + out * inverse * r.gain[...]).astype(BF)
        store(t).start()

    @pl.when(first)
    def _():
        @pl.loop(0, z.nb)
        def _(g):
            @pl.when(tail_chip)
            def _():
                r.ownm[g] = r.midq[g, z.chips - 1]

            @pl.when(jnp.logical_not(tail_chip))
            def _():
                own_mid(g, 0).wait_recv()

            own_grad(g, 0).wait_recv()
            r.final[:, g] = renormalize(r.ownm[g].astype(F32), r.og_r[g].astype(F32))

    @pl.when(second)
    def _():
        @pl.loop(0, z.nb)
        def _(g):
            total, middle = split(r.gsum[g + z.nb]), split(r.wb[g + z.nb, c].astype(F32))
            mine, base = total[:, 0], middle[:, 0]
            for t in range(1, z.chips):
                mine = jnp.where(p == t, total[:, t], mine)
                base = jnp.where(p == t, middle[:, t], base)
            for t in range(z.chips):
                @pl.when(p != t)
                def _():
                    cross_grad(g, t, t).wait_recv()
            for t in range(z.chips):
                mine = mine + jnp.where(p == t, 0.0, r.ox_r[g, t].astype(F32))
            r.final[:, g] = renormalize(base, mine)

    @pl.when(s < z.count - 1)
    def _():
        halo(0).wait_send()
        halo(1).wait_send()

    @pl.loop(0, z.ng)
    def _(g):
        pair(g).wait_send()

        @pl.when(either(both(first, p < z.chips - 1), both(second, p > 0, g < z.nb)))
        def _():
            chain(g).wait_send()

        @pl.when(both(first, tail_chip))
        def _():
            mid_out(g).wait_send()

        @pl.when(both(second, p < z.chips - 1))
        def _():
            mid_on(g).wait_send()

        @pl.when(second)
        def _():
            mid_part(g, c).wait_send()

    @pl.loop(0, z.nb)
    def _(g):
        for t in range(z.chips):
            if t < z.chips - 1:
                @pl.when(both(first, tail_chip))
                def _():
                    own_mid(g, t).wait_send()

            @pl.when(both(second, head_chip))
            def _():
                own_grad(g, t).wait_send()

            @pl.when(both(second, p != t))
            def _():
                cross_grad(g, t, p).wait_send()

    @pl.loop(0, z.rows // 256)
    def _(t):
        store(t).wait()


def shards(
    attn_query, attn_key, attn_value, fast_query, fast_key, fast_value, rates, fast_weights, gain
):
    rows, d = fast_key.shape
    f = fast_weights.shape[1]
    z = sizes(lax.axis_size("seq"), rows, d, f, attn_query.shape[1])
    weights = jnp.swapaxes(fast_weights[0], 0, 1).reshape(3, 2, z.chips, 2, z.nb, z.rpo, d)
    parts = scratch(z)
    anywhere = pl.BlockSpec(memory_space=pl.ANY)
    vmem = pl.BlockSpec(memory_space=pltpu.VMEM)
    mixed, final = pl.pallas_call(
        functools.partial(kernel, z, INPUTS + ("mixed", "final") + tuple(parts)),
        out_shape=(
            jax.ShapeDtypeStruct((rows, d), BF),
            jax.ShapeDtypeStruct((3, z.nb, z.rpo, d), F32),
        ),
        in_specs=[anywhere] * 6 + [vmem, anywhere, vmem],
        out_specs=(anywhere, vmem),
        scratch_shapes=list(parts.values()),
        compiler_params=pltpu.CompilerParams(
            vmem_limit_bytes=LIMIT, collective_id=0, has_side_effects=True
        ),
    )(
        attn_query, attn_key, attn_value, fast_query, fast_key, fast_value,
        rates.reshape(1, rows), weights, gain,
    )
    return (mixed, jnp.swapaxes(final.reshape(3, z.share, d), 0, 1)[None])


def solution(mesh):
    tokens = P("seq", "head")
    in_specs = (tokens,) * 7 + (P("head", None, None, None), P("head", None))
    out_specs = (tokens, P("head", "seq", None, None))
    return jax.shard_map(shards, mesh=mesh, in_specs=in_specs, out_specs=out_specs, check_vma=False)
```

```python
import contextlib
import functools
import math
from types import SimpleNamespace

import jax
import jax.numpy as jnp
from jax import lax
from jax.experimental import pallas as pl
from jax.experimental.pallas import tpu as pltpu
from jax.sharding import PartitionSpec as P

AH = 128
WINDOW = 512
EPSILON = 1e-06
NEG = -1e30
NT = (((1,), (1,)), ((), ()))
NN = (((1,), (0,)), ((), ()))
LIMIT = 52 * 1024 * 1024
UNIT = 32
PACK = 2
TILE = 1024
SMALL = 512
TRACE = False
BF = jnp.bfloat16
F32 = jnp.float32


def scope(name):
    return jax.named_scope(name) if TRACE else contextlib.nullcontext()


def mm(a, b, dims):
    return lax.dot_general(a, b, dims, preferred_element_type=jnp.float32)


def sigmoid(v):
    return 0.5 * jnp.tanh(0.5 * v) + 0.5


def attend_scores(q, keys, biases):
    rows = q.shape[0]
    old, mid, new = (mm(q, k, NT) for k in keys)
    if biases[0] is not None:
        old = old + biases[0]
    if biases[1] is not None:
        mid = mid + biases[1]
    row = lax.broadcasted_iota(jnp.int32, (rows, rows), 0)
    col = lax.broadcasted_iota(jnp.int32, (rows, rows), 1)
    causal = col <= row
    return jnp.where(causal, new, old), mid, causal


def attend_values(edge, mid, causal, values):
    factor = math.log2(math.e) / math.sqrt(AH)
    top = jnp.max(jnp.maximum(edge, mid), -1, keepdims=True)
    edge = jnp.exp2((edge - top) * factor)
    mid = jnp.exp2((mid - top) * factor)
    p_new = jnp.where(causal, edge, 0.0).astype(BF)
    p_old = jnp.where(causal, 0.0, edge).astype(BF)
    ones = jnp.ones_like(values[0])
    values = jnp.concatenate([jnp.concatenate([v, ones], 1) for v in values], 0)
    out = mm(jnp.concatenate([p_old, mid.astype(BF), p_new], 1), values, NN)
    return out[:, :AH] * (1.0 / out[:, AH:])


def renormalize(previous, grad):
    moved = previous + grad
    return moved * (
        jnp.sqrt(jnp.mean(previous * previous, axis=-1, keepdims=True) + EPSILON)
        / jnp.sqrt(jnp.mean(moved * moved, axis=-1, keepdims=True) + EPSILON)
    )


def sizes(count, rows, d, f, columns):
    half = count // 2
    chips = half // 2
    rpo = UNIT // chips
    share = f // count
    per_block = share // rpo
    groups = 2 * per_block
    z = SimpleNamespace(
        count=count, half=half, chips=chips, rpo=rpo, share=share, nb=per_block, ng=groups,
        ns=groups // PACK, rows=rows, d=d, heads=columns // AH,
    )
    assert z.rpo * z.chips == UNIT and z.nb * z.rpo == z.share and z.ns * PACK == z.ng
    assert z.heads == z.ns and z.ns >= 3 + (z.nb - 1) // PACK
    return z


def scratch(z):
    unit = (3, UNIT, z.d)
    piece = (3, z.rpo, z.d)
    tokens = pltpu.VMEM((z.rows, z.d), BF)
    halo = pltpu.VMEM((WINDOW, z.d), BF)
    dma = pltpu.SemaphoreType.DMA
    return dict(
        qs=tokens, ks=tokens, vs=tokens, fqs=tokens, xs=tokens, ys=tokens, hid=tokens, outs=tokens,
        att=pltpu.VMEM((z.rows, z.d), F32),
        hk=halo, hv=halo,
        rates=pltpu.VMEM((1, z.rows), F32), gains=pltpu.VMEM((1, z.d), F32),
        wf=pltpu.VMEM((z.ng, 2, 3, z.chips, z.rpo, z.d), F32),
        wb=pltpu.VMEM((z.ng, 2) + unit, BF),
        acc=pltpu.VMEM((PACK, 2) + unit, F32),
        gsum=pltpu.VMEM((z.ng,) + unit, F32),
        pair_s=pltpu.VMEM((z.ng,) + unit, BF),
        pair_r=pltpu.VMEM((z.ng,) + unit, BF),
        chain_s=pltpu.VMEM((z.ng,) + unit, BF),
        chain_r=pltpu.VMEM((z.ng,) + unit, BF),
        midb=pltpu.VMEM((z.ng,) + unit, BF),
        midq=pltpu.VMEM((z.nb, z.chips) + piece, BF),
        ownm=pltpu.VMEM((z.nb,) + piece, BF),
        og_s=pltpu.VMEM((z.nb, z.chips) + piece, BF),
        ox_s=pltpu.VMEM((z.nb, z.chips) + piece, BF),
        og_r=pltpu.VMEM((z.nb,) + piece, BF),
        ox_r=pltpu.VMEM((z.nb, z.chips) + piece, BF),
        load_sem=dma((8,)), store_sem=dma((z.rows // (2 * SMALL),)), wf_sem=dma((z.ng, 2)),
        halo_ss=dma((2,)), halo_rs=dma((2,)),
        pair_ss=dma((z.ng,)), pair_rs=dma((z.ng,)),
        chain_ss=dma((z.ng,)), chain_rs=dma((z.ng,)),
        mid_ss=dma((z.ng,)), mid_rs=dma((z.ng,)),
        part_ss=dma((z.ng,)), part_rs=dma((z.ng,)),
        om_ss=dma((z.nb, z.chips)), om_rs=dma((z.nb,)),
        og_ss=dma((z.nb, z.chips)), og_rs=dma((z.nb,)),
        ox_ss=dma((z.nb, z.chips)), ox_rs=dma((z.nb, z.chips)),
    )


INPUTS = ("q", "k", "v", "fq", "fk", "fv", "rate", "w", "gain")


def kernel(z, names, *refs):
    r = SimpleNamespace(**dict(zip(names, refs)))
    s = lax.axis_index("seq")
    hd = lax.axis_index("head")
    chip = lax.div(s, 2)
    c = s - 2 * chip
    b = lax.div(chip, z.chips)
    p = chip - b * z.chips
    first, second = b == 0, b == 1
    head_chip, tail_chip = p == 0, p == z.chips - 1

    def both(*conditions):
        return functools.reduce(jnp.logical_and, conditions)

    def either(*conditions):
        return functools.reduce(jnp.logical_or, conditions)

    def remote(src, dst, ss, rs, device):
        return pltpu.make_async_remote_copy(
            src_ref=src, dst_ref=dst, send_sem=ss, recv_sem=rs,
            device_id=(device, hd), device_id_type=pl.DeviceIdType.MESH,
        )

    def pair(g):
        return remote(r.pair_s.at[g], r.pair_r.at[g], r.pair_ss.at[g], r.pair_rs.at[g], s + 1 - 2 * c)

    def chain(g):
        return remote(r.chain_s.at[g], r.chain_r.at[g], r.chain_ss.at[g], r.chain_rs.at[g], s + 2 - 4 * b)

    def mid_out(g):
        return remote(r.midb.at[g], r.wb.at[g, c], r.mid_ss.at[g], r.mid_rs.at[g], s + 2)

    def mid_on(g):
        return remote(r.wb.at[g, c], r.wb.at[g, c], r.mid_ss.at[g], r.mid_rs.at[g], s + 2)

    def mid_part(g, core):
        return remote(r.wb.at[g, core], r.wb.at[g, core], r.part_ss.at[g], r.part_rs.at[g], s + 1 - 2 * c)

    def own_mid(g, t):
        return remote(r.midq.at[g, t], r.ownm.at[g], r.om_ss.at[g, t], r.om_rs.at[g], 2 * t + c)

    def own_grad(g, t):
        return remote(r.og_s.at[g, t], r.og_r.at[g], r.og_ss.at[g, t], r.og_rs.at[g], 2 * t + c)

    def cross_grad(g, t, origin):
        return remote(
            r.ox_s.at[g, t], r.ox_r.at[g, origin], r.ox_ss.at[g, t], r.ox_rs.at[g, origin],
            z.half + 2 * t + c,
        )

    def halo(n):
        src, dst = ((r.k, r.hk), (r.v, r.hv))[n]
        return remote(
            src.at[pl.ds(z.rows - WINDOW, WINDOW)], dst, r.halo_ss.at[n], r.halo_rs.at[n], s + 1
        )

    def load(n):
        src, dst = (
            (r.q, r.qs), (r.k, r.ks), (r.v, r.vs), (r.fq, r.fqs), (r.fk, r.xs), (r.fv, r.ys),
            (r.rate, r.rates), (r.gain, r.gains),
        )[n]
        return pltpu.make_async_copy(src, dst, r.load_sem.at[n])

    def load_w(g, core):
        block = lax.div(g, z.nb)
        return pltpu.make_async_copy(
            r.w.at[:, block, :, core, g - block * z.nb], r.wf.at[g, core], r.wf_sem.at[g, core]
        )

    def peer(n):
        other, core, block = n // 2, n % 2, n // z.half
        near = b == block
        if other < z.chips:
            near = either(near, chip == z.chips)
        if other == z.chips:
            near = either(near, first)
        return both(s != n, either(both(c == core, near), s == n - 1, s == n + 1))

    barrier = pltpu.get_barrier_semaphore()
    for n in range(z.count):
        @pl.when(peer(n))
        def _():
            pl.semaphore_signal(
                barrier, inc=1, device_id=(n, hd), device_id_type=pl.DeviceIdType.MESH
            )

    def load_weights(low, high):
        @pl.loop(low, high)
        def _(g):
            for core in range(2):
                load_w(g, core).start()

    @pl.when(first)
    def _():
        load_weights(0, PACK)
        for n in (4, 6, 5):
            load(n).start()

    @pl.when(second)
    def _():
        for n in (1, 0, 2, 6):
            load(n).start()

    load(7).start()

    @pl.when(s == 0)
    def _():
        r.hk[...] = jnp.zeros_like(r.hk)
        r.hv[...] = jnp.zeros_like(r.hv)

    late_key = both(first, c == 1, p < z.chips - 1)
    late_value = both(first, c == 1)

    def enter():
        pl.semaphore_wait(barrier, sum(jnp.where(peer(n), 1, 0) for n in range(z.count)))

        @pl.when(both(s < z.count - 1, jnp.logical_not(late_key)))
        def _():
            halo(0).start()

        @pl.when(both(s < z.count - 1, jnp.logical_not(late_value)))
        def _():
            halo(1).start()

        @pl.when(first)
        def _():
            for n in (0, 1, 2, 3):
                load(n).start()

        @pl.when(second)
        def _():
            for n in (4, 5, 3):
                load(n).start()

        load(7).wait()

    def weights(i):
        w = r.wb[pl.ds(i * PACK, PACK)].reshape(PACK * 2, 3, UNIT, z.d)
        return w

    def grad_step(i):
        n = PACK * 2
        w = weights(i)
        w_gu = w[:, 0:2].reshape(n * 2 * UNIT, z.d)
        w_down = w[:, 2].reshape(n * UNIT, z.d)
        tiles = z.rows // TILE

        def rows(ref, t):
            return ref[t * TILE : (t + 1) * TILE, :]

        def products(t):
            return mm(w_gu, rows(r.xs, t), NT), mm(w_down, rows(r.ys, t), NT)

        ahead = products(0)
        for t in range(tiles):
            gu, back = ahead
            if t + 1 < tiles:
                ahead = products(t + 1)
            rate = r.rates[:, t * TILE : (t + 1) * TILE]
            gu = gu.reshape(n, 2, UNIT, TILE)
            back = back * rate
            gate = gu[:, 0].reshape(n * UNIT, TILE)
            up = gu[:, 1].reshape(n * UNIT, TILE)
            sg = sigmoid(gate)
            active = gate * sg
            hidden = (active * up * rate).astype(BF)
            up_grad = (back * active).astype(BF)
            gate_grad = (back * up * (sg * (1.0 + gate * (1.0 - sg)))).astype(BF)
            both_grad = jnp.concatenate(
                [gate_grad.reshape(n, 1, UNIT, TILE), up_grad.reshape(n, 1, UNIT, TILE)], 1
            ).reshape(n * 2 * UNIT, TILE)
            wide = mm(both_grad, rows(r.xs, t), NN).reshape(PACK, 2, 2, UNIT, z.d)
            down = mm(hidden, rows(r.ys, t), NN).reshape(PACK, 2, UNIT, z.d)
            if t == 0:
                r.acc[:, :, 0:2] = wide
                r.acc[:, :, 2] = down
            else:
                r.acc[:, :, 0:2] += wide
                r.acc[:, :, 2] += down
        for k in range(PACK):
            g = i * PACK + k
            r.gsum[g] = r.acc[k, c]
            r.pair_s[g] = r.acc[k, 1 - c].astype(BF)

    def combine(g):
        pair(g).wait_recv()
        r.gsum[g] += r.pair_r[g].astype(F32)

    def add_chain(g):
        chain(g).wait_recv()
        r.gsum[g] += r.chain_r[g].astype(F32)

    def send_chain(g):
        r.chain_s[g] = r.gsum[g].astype(BF)
        chain(g).start()

    def split(unit):
        return unit.reshape(3, z.chips, z.rpo, z.d)

    def reduce_first(i):
        for k in range(PACK):
            g = i * PACK + k
            combine(g)

            @pl.when(p > 0)
            def _():
                add_chain(g)

            send_chain(g)

    def make_middle(i):
        for k in range(PACK):
            g = i * PACK + k
            combine(g)
            add_chain(g)
            middle = renormalize(r.wf[g, c].reshape(3, UNIT, z.d), r.gsum[g])
            r.midb[g] = middle.astype(BF)
            mid_out(g).start()

            @pl.when(g < z.nb)
            def _():
                pieces = split(middle)
                for t in range(z.chips):
                    r.midq[g, t] = pieces[:, t].astype(BF)
                    if t < z.chips - 1:
                        own_mid(g, t).start()

    def relay(g):
        mid_on(g).wait_recv()

        @pl.when(p < z.chips - 1)
        def _():
            mid_on(g).start()

        mid_part(g, c).start()

    def reduce_second(i):
        for k in range(PACK):
            g = i * PACK + k
            combine(g)

            @pl.when(both(g < z.nb, tail_chip))
            def _():
                send_chain(g)

            @pl.when(g >= z.nb)
            def _():
                pieces = split(r.gsum[g])
                for t in range(z.chips):
                    @pl.when(p != t)
                    def _():
                        r.ox_s[g - z.nb, t] = pieces[:, t].astype(BF)

                    @pl.when(p > t)
                    def _():
                        cross_grad(g - z.nb, t, p).start()

    def hand_back(i):
        for k in range(PACK):
            g = i * PACK + k

            @pl.when(g < z.nb)
            def _():
                add_chain(g)

                @pl.when(p > 0)
                def _():
                    send_chain(g)

                @pl.when(head_chip)
                def _():
                    pieces = split(r.gsum[g])
                    for t in range(z.chips):
                        r.og_s[g, t] = pieces[:, t].astype(BF)
                        own_grad(g, t).start()

    tile = WINDOW // 2

    def attention_tiles(h, tiles, bias):
        columns = pl.ds(pl.multiple_of(h * AH, AH), AH)

        def block(ref, halo_ref, at):
            if at < 0:
                return halo_ref[(at + 2) * tile : (at + 3) * tile, columns]
            return ref[at * tile : (at + 1) * tile, columns]

        def scores(t):
            keys = [block(r.ks, r.hk, t - 2 + n) for n in range(3)]
            biases = [bias if t - 2 + n < 0 else None for n in range(2)]
            return attend_scores(r.qs[t * tile : (t + 1) * tile, columns], keys, biases)

        ahead = scores(tiles[0])
        for n, t in enumerate(tiles):
            now = ahead
            if n + 1 < len(tiles):
                ahead = scores(tiles[n + 1])
            values = [block(r.vs, r.hv, t - 2 + m) for m in range(3)]
            r.att[t * tile : (t + 1) * tile, columns] = attend_values(*now, values)

    def hidden_step(i):
        n = PACK * 2 * UNIT
        w = weights(i)
        w_gu = jnp.concatenate([w[:, 0].reshape(n, z.d), w[:, 1].reshape(n, z.d)], 0)
        columns = pl.ds(pl.multiple_of(i * n, n), n)
        tiles = z.rows // SMALL

        def products(t):
            return mm(r.fqs[t * SMALL : (t + 1) * SMALL, :], w_gu, NT)

        ahead = products(0)
        for t in range(tiles):
            now = ahead
            if t + 1 < tiles:
                ahead = products(t + 1)
            gate, up = now[:, :n], now[:, n:]
            r.hid[t * SMALL : (t + 1) * SMALL, columns] = (gate * sigmoid(gate) * up).astype(BF)

    @pl.loop(0, 2 * z.ns)
    def _(j):
        early, late = j < z.ns, j >= z.ns
        i = lax.rem(j, z.ns)

        @pl.when(either(both(first, j == 0), both(second, j == z.ns)))
        def _():
            for n in (4, 5, 6):
                load(n).wait()

        @pl.when(either(both(second, j == 0), both(first, j == z.ns)))
        def _():
            for n in (0, 1, 2):
                load(n).wait()

        @pl.when(j == z.ns)
        def _():
            load(3).wait()

        @pl.when(both(first, early))
        def _():
            for k in range(PACK):
                g = i * PACK + k
                for core in range(2):
                    load_w(g, core).wait()
                    r.wb[g, core] = r.wf[g, core].reshape(3, UNIT, z.d).astype(BF)

            @pl.when(j == 0)
            def _():
                load_weights(PACK, z.ng)

        differentiate = first == early

        @pl.when(differentiate)
        def _():
            with scope("grad"):
                grad_step(i)

        @pl.when(jnp.logical_not(differentiate))
        def _():
            with scope("att"):
                attention_tiles(i, range(2, z.rows // tile), None)

        @pl.when(j == 0)
        def _():
            with scope("enter"):
                enter()

        @pl.when(differentiate)
        def _():
            for k in range(PACK):
                pair(i * PACK + k).start()

        @pl.when(both(first, p < z.chips - 1, early))
        def _():
            with scope("rfirst"):
                reduce_first(i)

        @pl.when(both(second, late, j < 2 * z.ns - 1))
        def _():
            with scope("relay0"):
                relay((i + 1) * PACK)

        @pl.when(both(late_key, j == z.ns + 1))
        def _():
            halo(0).start()

        @pl.when(both(late_value, j == jnp.where(p < z.chips - 1, z.ns + 2, z.ns + 3)))
        def _():
            halo(1).start()

        @pl.when(late)
        def _():
            with scope("hidden"):
                hidden_step(i)

        @pl.when(both(second, late, j < 2 * z.ns - 1))
        def _():
            for k in range(1, PACK):
                with scope("relay1"):
                    relay((i + 1) * PACK + k)

        @pl.when(both(first, tail_chip, either(j == 2, both(j >= 4, j < 3 + z.ns))))
        def _():
            with scope("middle"):
                make_middle(jnp.where(j == 2, 0, j - 3))

        @pl.when(both(second, late))
        def _():
            with scope("rsecond"):
                reduce_second(i)

        @pl.when(both(second, j == 2 * z.ns - 1))
        def _():
            for t in range(1, z.chips):
                @pl.when(p < t)
                def _():
                    @pl.loop(0, z.nb)
                    def _(g):
                        cross_grad(g, t, p).start()

        @pl.when(both(second, p < z.chips - 1, j >= z.ns + 2))
        def _():
            with scope("handback"):
                hand_back(j - z.ns - 2)

        waits = either(first, s == z.half)

        @pl.when(j == jnp.where(waits, 2 * z.ns - 1, z.ns - 1))
        def _():
            @pl.when(s > 0)
            def _():
                with scope("halow"):
                    halo(0).wait_recv()
                    halo(1).wait_recv()

            bias = jnp.where(s == 0, jnp.float32(NEG), jnp.float32(0.0))

            @pl.loop(0, z.heads)
            def _(h):
                with scope("atth"):
                    attention_tiles(h, range(2), bias)

        @pl.when(both(second, j >= z.ns - 1, j < 2 * z.ns - 1))
        def _():
            base = (j + 1 - z.ns) * PACK

            @pl.when(j == z.ns - 1)
            def _():
                relay(base)

                for k in range(1, PACK):
                    relay(base + k)

            with scope("partw"):
                for k in range(PACK):
                    mid_part(base + k, 1 - c).wait_recv()

    w_down = r.wb[:, :, 2].reshape(z.ng * 2 * UNIT, z.d)

    def store(t):
        at = pl.ds(pl.multiple_of(t * 2 * SMALL, 2 * SMALL), 2 * SMALL)
        return pltpu.make_async_copy(r.outs.at[at], r.mixed.at[at], r.store_sem.at[t])

    @pl.loop(0, z.rows // (2 * SMALL))
    def _(t):
        spots = [pl.ds(pl.multiple_of(t * 2 * SMALL + n * SMALL, SMALL), SMALL) for n in range(2)]
        with scope("down"):
            outs = [mm(r.hid[at, :], w_down, NN) for at in spots]
            for at, out in zip(spots, outs):
                inverse = lax.rsqrt(jnp.mean(out * out, axis=-1, keepdims=True) + EPSILON)
                r.outs[at, :] = (r.att[at, :] + out * inverse * r.gains[...]).astype(BF)
        store(t).start()

    @pl.when(first)
    def _():
        @pl.loop(0, z.nb)
        def _(g):
            @pl.when(tail_chip)
            def _():
                r.ownm[g] = r.midq[g, z.chips - 1]

            @pl.when(jnp.logical_not(tail_chip))
            def _():
                with scope("ownmw"):
                    own_mid(g, 0).wait_recv()

            with scope("owngw"):
                own_grad(g, 0).wait_recv()
            r.final[:, g] = renormalize(r.ownm[g].astype(F32), r.og_r[g].astype(F32))

    @pl.when(second)
    def _():
        @pl.loop(0, z.nb)
        def _(g):
            total, middle = split(r.gsum[g + z.nb]), split(r.wb[g + z.nb, c].astype(F32))
            mine, base = total[:, 0], middle[:, 0]
            for t in range(1, z.chips):
                mine = jnp.where(p == t, total[:, t], mine)
                base = jnp.where(p == t, middle[:, t], base)
            for t in range(z.chips):
                @pl.when(p != t)
                def _():
                    with scope("crossw"):
                        cross_grad(g, t, t).wait_recv()
            for t in range(z.chips):
                mine = mine + jnp.where(p == t, 0.0, r.ox_r[g, t].astype(F32))
            r.final[:, g] = renormalize(base, mine)

    @pl.when(s < z.count - 1)
    def _():
        halo(0).wait_send()
        halo(1).wait_send()

    @pl.loop(0, z.ng)
    def _(g):
        with scope("sendw"):
            pair(g).wait_send()

        @pl.when(either(both(first, p < z.chips - 1), both(second, p > 0, g < z.nb)))
        def _():
            chain(g).wait_send()

        @pl.when(both(first, tail_chip))
        def _():
            mid_out(g).wait_send()

        @pl.when(both(second, p < z.chips - 1))
        def _():
            mid_on(g).wait_send()

        @pl.when(second)
        def _():
            mid_part(g, c).wait_send()

    @pl.loop(0, z.nb)
    def _(g):
        for t in range(z.chips):
            if t < z.chips - 1:
                @pl.when(both(first, tail_chip))
                def _():
                    own_mid(g, t).wait_send()

            @pl.when(both(second, head_chip))
            def _():
                own_grad(g, t).wait_send()

            @pl.when(both(second, p != t))
            def _():
                cross_grad(g, t, p).wait_send()

    @pl.loop(0, z.rows // (2 * SMALL))
    def _(t):
        with scope("storew"):
            store(t).wait()


def shards(
    attn_query, attn_key, attn_value, fast_query, fast_key, fast_value, rates, fast_weights, gain
):
    rows, d = fast_key.shape
    f = fast_weights.shape[1]
    z = sizes(lax.axis_size("seq"), rows, d, f, attn_query.shape[1])
    weights = jnp.swapaxes(fast_weights[0], 0, 1).reshape(3, 2, z.chips, 2, z.nb, z.rpo, d)
    parts = scratch(z)
    anywhere = pl.BlockSpec(memory_space=pl.ANY)
    vmem = pl.BlockSpec(memory_space=pltpu.VMEM)
    mixed, final = pl.pallas_call(
        functools.partial(kernel, z, INPUTS + ("mixed", "final") + tuple(parts)),
        out_shape=(
            jax.ShapeDtypeStruct((rows, d), BF),
            jax.ShapeDtypeStruct((3, z.nb, z.rpo, d), F32),
        ),
        in_specs=[anywhere] * 9,
        out_specs=(anywhere, vmem),
        scratch_shapes=list(parts.values()),
        compiler_params=pltpu.CompilerParams(
            vmem_limit_bytes=LIMIT, collective_id=0, has_side_effects=True
        ),
    )(
        attn_query, attn_key, attn_value, fast_query, fast_key, fast_value,
        rates.reshape(1, rows), weights, gain,
    )
    return (mixed, jnp.swapaxes(final.reshape(3, z.share, d), 0, 1)[None])


def solution(mesh):
    tokens = P("seq", "head")
    in_specs = (tokens,) * 7 + (P("head", None, None, None), P("head", None))
    out_specs = (tokens, P("head", "seq", None, None))
    return jax.shard_map(shards, mesh=mesh, in_specs=in_specs, out_specs=out_specs, check_vma=False)
```

```python
import contextlib
import functools
import math
from types import SimpleNamespace

import jax
import jax.numpy as jnp
from jax import lax
from jax.experimental import pallas as pl
from jax.experimental.pallas import tpu as pltpu
from jax.sharding import PartitionSpec as P

AH = 128
WINDOW = 512
EPSILON = 1e-06
NEG = -1e30
NT = (((1,), (1,)), ((), ()))
NN = (((1,), (0,)), ((), ()))
LIMIT = 67043328
UNIT = 32
PACK = 2
TILE = 1024
SMALL = 512
TRACE = False
PIECES = 4
BF = jnp.bfloat16
F32 = jnp.float32


def scope(name):
    return jax.named_scope(name) if TRACE else contextlib.nullcontext()


def mm(a, b, dims):
    return lax.dot_general(a, b, dims, preferred_element_type=jnp.float32)


def sigmoid(v):
    return 0.5 * jnp.tanh(0.5 * v) + 0.5


def attend_scores(q, keys, biases):
    rows = q.shape[0]
    old, mid, new = (mm(q, k, NT) for k in keys)
    if biases[0] is not None:
        old = old + biases[0]
    if biases[1] is not None:
        mid = mid + biases[1]
    row = lax.broadcasted_iota(jnp.int32, (rows, rows), 0)
    col = lax.broadcasted_iota(jnp.int32, (rows, rows), 1)
    causal = col <= row
    return jnp.where(causal, new, old), mid, causal


def attend_values(edge, mid, causal, values):
    factor = math.log2(math.e) / math.sqrt(AH)
    top = jnp.max(jnp.maximum(edge, mid), -1, keepdims=True)
    edge = jnp.exp2((edge - top) * factor)
    mid = jnp.exp2((mid - top) * factor)
    p_new = jnp.where(causal, edge, 0.0).astype(BF)
    p_old = jnp.where(causal, 0.0, edge).astype(BF)
    ones = jnp.ones_like(values[0])
    values = jnp.concatenate([jnp.concatenate([v, ones], 1) for v in values], 0)
    out = mm(jnp.concatenate([p_old, mid.astype(BF), p_new], 1), values, NN)
    return out[:, :AH] * (1.0 / out[:, AH:])


def renormalize(previous, grad):
    moved = previous + grad
    return moved * (
        jnp.sqrt(jnp.mean(previous * previous, axis=-1, keepdims=True) + EPSILON)
        / jnp.sqrt(jnp.mean(moved * moved, axis=-1, keepdims=True) + EPSILON)
    )


def sizes(count, rows, d, f, columns):
    half = count // 2
    chips = half // 2
    rpo = UNIT // chips
    share = f // count
    per_block = share // rpo
    groups = 2 * per_block
    z = SimpleNamespace(
        count=count, half=half, chips=chips, rpo=rpo, share=share, nb=per_block, ng=groups,
        ns=groups // PACK, rows=rows, d=d, heads=columns // AH,
    )
    assert z.rpo * z.chips == UNIT and z.nb * z.rpo == z.share and z.ns * PACK == z.ng
    assert z.heads == z.ns and z.ng == 2 * z.ns and z.ns == 5 and z.rows == 2 * TILE
    return z


def scratch(z):
    unit = (3, UNIT, z.d)
    piece = (3, z.rpo, z.d)
    tokens = pltpu.VMEM((z.rows, z.d), BF)
    halo = pltpu.VMEM((WINDOW, z.d), BF)
    dma = pltpu.SemaphoreType.DMA
    return dict(
        qs=tokens, ks=tokens, vs=tokens, fqs=tokens, xs=tokens, ys=tokens, hid=tokens, outs=tokens,
        att=pltpu.VMEM((z.rows, z.d), F32),
        hk=halo, hv=halo,
        rates=pltpu.VMEM((1, z.rows), F32), gains=pltpu.VMEM((1, z.d), F32),
        wf=pltpu.VMEM((z.ng, 2, 3, z.chips, z.rpo, z.d), F32),
        wb=pltpu.VMEM((z.ng, 2) + unit, BF),
        acc=pltpu.VMEM((PACK, 2) + unit, F32),
        gsum=pltpu.VMEM((z.ng,) + unit, F32),
        pair_s=pltpu.VMEM((z.ng,) + unit, BF),
        pair_r=pltpu.VMEM((z.ng,) + unit, BF),
        chain_s=pltpu.VMEM((z.ng,) + unit, BF),
        chain_r=pltpu.VMEM((z.ng,) + unit, BF),
        midb=pltpu.VMEM((z.ng,) + unit, BF),
        midq=pltpu.VMEM((z.nb, z.chips) + piece, BF),
        ownm=pltpu.VMEM((z.nb,) + piece, BF),
        og_s=pltpu.VMEM((z.nb, z.chips) + piece, BF),
        ox_s=pltpu.VMEM((z.nb, z.chips) + piece, BF),
        og_r=pltpu.VMEM((z.nb,) + piece, BF),
        ox_r=pltpu.VMEM((z.nb, z.chips) + piece, BF),
        rows_out=pltpu.VMEM((z.nb, 3, z.rpo, z.d), F32), rows_sem=dma((1,)), load_sem=dma((10,)), store_sem=dma((1,)), wf_sem=dma((z.ns,)),
        halo_ss=dma((4,)), halo_rs=dma((4,)),
        pair_ss=dma((1,)), pair_rs=dma((z.ng,)),
        chain_ss=dma((1,)), chain_rs=dma((z.ng,)),
        mid_ss=dma((1,)), mid_rs=dma((z.ng,)),
        part_ss=dma((1,)), part_rs=dma((z.ng,)),
        om_ss=dma((1,)), om_rs=dma((z.nb,)),
        og_ss=dma((1,)), og_rs=dma((z.nb,)),
        ox_ss=dma((1,)), ox_rs=dma((z.nb, z.chips)),
    )


INPUTS = ("q", "k", "v", "fq", "fk", "fv", "rate", "w", "gain")


def kernel(z, names, *refs):
    r = SimpleNamespace(**dict(zip(names, refs)))
    s = lax.axis_index("seq")
    hd = lax.axis_index("head")
    chip = lax.div(s, 2)
    c = s - 2 * chip
    b = lax.div(chip, z.chips)
    p = chip - b * z.chips
    first, second = b == 0, b == 1
    head_chip, tail_chip = p == 0, p == z.chips - 1

    def both(*conditions):
        return functools.reduce(jnp.logical_and, conditions)

    def either(*conditions):
        return functools.reduce(jnp.logical_or, conditions)

    def remote(src, dst, ss, rs, device):
        return pltpu.make_async_remote_copy(
            src_ref=src, dst_ref=dst, send_sem=ss, recv_sem=rs,
            device_id=(device, hd), device_id_type=pl.DeviceIdType.MESH,
        )

    def pair(g):
        return remote(r.pair_s.at[g], r.pair_r.at[g], r.pair_ss.at[0], r.pair_rs.at[g], s + 1 - 2 * c)

    def chain(g):
        return remote(r.chain_s.at[g], r.chain_r.at[g], r.chain_ss.at[0], r.chain_rs.at[g], s + 2 - 4 * b)

    def mid_out(g):
        return remote(r.midb.at[g], r.wb.at[g, c], r.mid_ss.at[0], r.mid_rs.at[g], s + 2)

    def mid_on(g):
        return remote(r.wb.at[g, c], r.wb.at[g, c], r.mid_ss.at[0], r.mid_rs.at[g], s + 2)

    def mid_part(g, core):
        return remote(r.wb.at[g, core], r.wb.at[g, core], r.part_ss.at[0], r.part_rs.at[g], s + 1 - 2 * c)

    def own_mid(g, t):
        return remote(r.midq.at[g, t], r.ownm.at[g], r.om_ss.at[0], r.om_rs.at[g], 2 * t + c)

    def own_grad(g, t):
        return remote(r.og_s.at[g, t], r.og_r.at[g], r.og_ss.at[0], r.og_rs.at[g], 2 * t + c)

    def cross_grad(g, t, origin):
        return remote(
            r.ox_s.at[g, t], r.ox_r.at[g, origin], r.ox_ss.at[0], r.ox_rs.at[g, origin],
            z.half + 2 * t + c,
        )

    def halo(n):
        src, dst = ((r.k, r.hk), (r.v, r.hv))[n // 2]
        half = WINDOW // 2
        start = n % 2 * half
        return remote(
            src.at[pl.ds(z.rows - WINDOW + start, half)], dst.at[pl.ds(start, half)],
            r.halo_ss.at[n], r.halo_rs.at[n], s + 1,
        )

    def load(n):
        src, dst = (
            (r.q, r.qs), (r.k, r.ks), (r.v, r.vs), (r.fq, r.fqs), (r.rate, r.rates), (r.gain, r.gains),
        )[n]
        return pltpu.make_async_copy(src, dst, r.load_sem.at[n + n // 4 * 2])

    def load_rows(n, half):
        src, dst = ((r.fk, r.xs), (r.fv, r.ys))[n]
        at = pl.ds(half * TILE, TILE)
        return pltpu.make_async_copy(src.at[at], dst.at[at], r.load_sem.at[4 + n + 4 * half])

    def load_w(g, core):
        block = lax.div(g, z.nb)
        return pltpu.make_async_copy(
            r.w.at[:, block, :, core, g - block * z.nb], r.wf.at[g, core], r.wf_sem.at[lax.div(g, PACK)]
        )

    def peer(n):
        other, core, block = n // 2, n % 2, n // z.half
        near = b == block
        if other < z.chips:
            near = either(near, chip == z.chips)
        if other == z.chips:
            near = either(near, first)
        return both(s != n, either(both(c == core, near), s == n - 1, s == n + 1))

    barrier = pltpu.get_barrier_semaphore()
    for n in range(z.count):
        @pl.when(peer(n))
        def _():
            pl.semaphore_signal(
                barrier, inc=1, device_id=(n, hd), device_id_type=pl.DeviceIdType.MESH
            )

    def load_weights(low, high):
        @pl.loop(low, high)
        def _(g):
            for core in range(2):
                load_w(g, core).start()

    @pl.when(first)
    def _():
        load_weights(0, PACK)
        load(4).start()
        for half in range(2):
            for n in range(2):
                load_rows(n, half).start()

    @pl.when(second)
    def _():
        for n in (1, 0, 2, 4):
            load(n).start()

    load(5).start()

    @pl.when(s == 0)
    def _():
        r.hk[...] = jnp.zeros_like(r.hk)
        r.hv[...] = jnp.zeros_like(r.hv)

    sends = s < z.count - 1
    border = both(first, c == 1, tail_chip)
    slow = both(first, c == 1, p < z.chips - 1)
    beside = both(first, c == 0)

    def start_halo(condition, parts):
        @pl.when(both(sends, condition))
        def _():
            for n in parts:
                halo(n).start()

    def enter():
        pl.semaphore_wait(barrier, sum(jnp.where(peer(n), 1, 0) for n in range(z.count)))

        start_halo(second, range(4))
        start_halo(border, (0, 1))
        start_halo(slow, (1,))

        load(5).wait()

    def load_rest():
        @pl.when(first)
        def _():
            for n in (0, 1, 2, 3):
                load(n).start()

        @pl.when(second)
        def _():
            for half in range(2):
                for n in range(2):
                    load_rows(n, half).start()
            load(3).start()

    def weights(i):
        w = r.wb[pl.ds(i * PACK, PACK)].reshape(PACK * 2, 3, UNIT, z.d)
        return w

    def grad_step(i, between):
        n = PACK * 2
        w = weights(i)
        w_gu = w[:, 0:2].reshape(n * 2 * UNIT, z.d)
        w_down = w[:, 2].reshape(n * UNIT, z.d)
        tiles = z.rows // TILE

        def rows(ref, t):
            return ref[t * TILE : (t + 1) * TILE, :]

        def products(t):
            return mm(w_gu, rows(r.xs, t), NT), mm(w_down, rows(r.ys, t), NT)

        for t in range(tiles):
            if t == 1:
                between()
            gu, back = products(t)
            rate = r.rates[:, t * TILE : (t + 1) * TILE]
            gu = gu.reshape(n, 2, UNIT, TILE)
            back = back * rate
            gate = gu[:, 0].reshape(n * UNIT, TILE)
            up = gu[:, 1].reshape(n * UNIT, TILE)
            sg = sigmoid(gate)
            active = gate * sg
            hidden = (active * up * rate).astype(BF)
            up_grad = (back * active).astype(BF)
            gate_grad = (back * up * (sg * (1.0 + gate * (1.0 - sg)))).astype(BF)
            both_grad = jnp.concatenate(
                [gate_grad.reshape(n, 1, UNIT, TILE), up_grad.reshape(n, 1, UNIT, TILE)], 1
            ).reshape(n * 2 * UNIT, TILE)
            wide = mm(both_grad, rows(r.xs, t), NN).reshape(PACK, 2, 2, UNIT, z.d)
            down = mm(hidden, rows(r.ys, t), NN).reshape(PACK, 2, UNIT, z.d)
            if t == 0:
                r.acc[:, :, 0:2] = wide
                r.acc[:, :, 2] = down
            else:
                r.acc[:, :, 0:2] += wide
                r.acc[:, :, 2] += down
        for k in range(PACK):
            g = i * PACK + k
            r.gsum[g] = r.acc[k, c]
            r.pair_s[g] = r.acc[k, 1 - c].astype(BF)

    def combine(g):
        pair(g).wait_recv()
        r.gsum[g] += r.pair_r[g].astype(F32)

    def add_chain(g):
        chain(g).wait_recv()
        r.gsum[g] += r.chain_r[g].astype(F32)

    def send_chain(g):
        r.chain_s[g] = r.gsum[g].astype(BF)
        chain(g).start()

    def split(unit):
        return unit.reshape(3, z.chips, z.rpo, z.d)

    def reduce_first(i):
        for k in range(PACK):
            g = i * PACK + k
            combine(g)

            @pl.when(p > 0)
            def _():
                add_chain(g)

            send_chain(g)

    def make_middle(g):
        combine(g)
        add_chain(g)
        middle = renormalize(r.wf[g, c].reshape(3, UNIT, z.d), r.gsum[g])
        r.midb[g] = middle.astype(BF)
        mid_out(g).start()

        @pl.when(g < z.nb)
        def _():
            pieces = split(middle)
            for t in range(z.chips):
                r.midq[g, t] = pieces[:, t].astype(BF)
                if t < z.chips - 1:
                    own_mid(g, t).start()

    def relay(g):
        mid_on(g).wait_recv()

        @pl.when(p < z.chips - 1)
        def _():
            mid_on(g).start()

        mid_part(g, c).start()

    def reduce_second(i):
        for k in range(PACK):
            g = i * PACK + k
            combine(g)

            @pl.when(both(g < z.nb, tail_chip))
            def _():
                send_chain(g)

            @pl.when(g >= z.nb)
            def _():
                pieces = split(r.gsum[g])
                for t in range(z.chips):
                    @pl.when(p != t)
                    def _():
                        r.ox_s[g - z.nb, t] = pieces[:, t].astype(BF)

                    @pl.when(p > t)
                    def _():
                        cross_grad(g - z.nb, t, p).start()

    def hand_back(i):
        for k in range(PACK):
            g = i * PACK + k

            @pl.when(g < z.nb)
            def _():
                add_chain(g)

                @pl.when(p > 0)
                def _():
                    send_chain(g)

                @pl.when(head_chip)
                def _():
                    pieces = split(r.gsum[g])
                    for t in range(z.chips):
                        r.og_s[g, t] = pieces[:, t].astype(BF)
                        own_grad(g, t).start()

    tile = WINDOW // 2

    def attention_tiles(h, tiles, bias):
        columns = pl.ds(pl.multiple_of(h * AH, AH), AH)

        def block(ref, halo_ref, at):
            if at < 0:
                return halo_ref[(at + 2) * tile : (at + 3) * tile, columns]
            return ref[at * tile : (at + 1) * tile, columns]

        def scores(t):
            keys = [block(r.ks, r.hk, t - 2 + n) for n in range(3)]
            biases = [bias if t - 2 + n < 0 else None for n in range(2)]
            return attend_scores(r.qs[t * tile : (t + 1) * tile, columns], keys, biases)

        ahead = scores(tiles[0])
        for n, t in enumerate(tiles):
            now = ahead
            if n + 1 < len(tiles):
                ahead = scores(tiles[n + 1])
            values = [block(r.vs, r.hv, t - 2 + m) for m in range(3)]
            r.att[t * tile : (t + 1) * tile, columns] = attend_values(*now, values)

    def hidden_step(i):
        n = PACK * 2 * UNIT
        w = weights(i)
        w_gu = jnp.concatenate([w[:, 0].reshape(n, z.d), w[:, 1].reshape(n, z.d)], 0)
        columns = pl.ds(pl.multiple_of(i * n, n), n)
        tiles = z.rows // SMALL

        def products(t):
            return mm(r.fqs[t * SMALL : (t + 1) * SMALL, :], w_gu, NT)

        ahead = products(0)
        for t in range(tiles):
            now = ahead
            if t + 1 < tiles:
                ahead = products(t + 1)
            gate, up = now[:, :n], now[:, n:]
            r.hid[t * SMALL : (t + 1) * SMALL, columns] = (gate * sigmoid(gate) * up).astype(BF)

    waits = either(first, s == z.half)

    def halo_tiles():
        @pl.when(s > 0)
        def _():
            with scope("halow"):
                for n in range(4):
                    halo(n).wait_recv()

        bias = jnp.where(s == 0, jnp.float32(NEG), jnp.float32(0.0))

        @pl.loop(0, z.heads)
        def _(h):
            with scope("atth"):
                attention_tiles(h, range(2), bias)

    @pl.loop(0, 2 * z.ns)
    def _(j):
        early, late = j < z.ns, j >= z.ns
        i = lax.rem(j, z.ns)

        @pl.when(either(both(first, j == 0), both(second, j == z.ns)))
        def _():
            load(4).wait()
            for n in range(2):
                load_rows(n, 0).wait()

        @pl.when(either(both(second, j == 0), both(first, j == z.ns)))
        def _():
            for n in (0, 1, 2):
                load(n).wait()

        @pl.when(j == z.ns)
        def _():
            load(3).wait()

        @pl.when(both(second, j == 0))
        def _():
            with scope("enter"):
                enter()

        @pl.when(both(first, early))
        def _():
            step = r.wf.at[pl.ds(i * PACK, PACK)]
            pltpu.make_async_copy(step, step, r.wf_sem.at[i]).wait()
            for k in range(PACK):
                g = i * PACK + k
                for core in range(2):
                    r.wb[g, core] = r.wf[g, core].reshape(3, UNIT, z.d).astype(BF)

            @pl.when(j == 0)
            def _():
                load_weights(PACK, z.ng)

        @pl.when(j == 1)
        def _():
            load_rest()

        differentiate = first == early

        def relay_next(k, ready):
            @pl.when(both(second, late, j < 2 * z.ns - 1, ready))
            def _():
                with scope("relay%d" % k):
                    relay((i + 1) * PACK + k)

        def between():
            @pl.when(either(both(first, j == 0), both(second, j == z.ns)))
            def _():
                for n in range(2):
                    load_rows(n, 1).wait()

            @pl.when(both(first, j == 0))
            def _():
                with scope("enter"):
                    enter()

            relay_next(0, both(i > 0, p < z.chips - 1))

            @pl.when(both(second, p < z.chips - 1, j >= z.ns + 3))
            def _():
                with scope("handback"):
                    hand_back(j - z.ns - 3)

            @pl.when(both(first, tail_chip, either(j == z.ns - 2, j == z.ns - 1)))
            def _():
                with scope("middle"):
                    make_middle(j - 1)

        def send_forward(low, high):
            @pl.when(both(second, j == 2 * z.ns - 1))
            def _():
                for t in range(1, z.chips):
                    @pl.when(p < t)
                    def _():
                        @pl.loop(low, high)
                        def _(g):
                            cross_grad(g, t, p).start()

        @pl.when(differentiate)
        def _():
            with scope("grad"):
                grad_step(i, between)

        @pl.when(jnp.logical_not(differentiate))
        def _():
            with scope("att"):
                attention_tiles(i, range(2, z.rows // tile), None)

        @pl.when(differentiate)
        def _():
            for k in range(PACK):
                pair(i * PACK + k).start()

        @pl.when(both(first, p < z.chips - 1, early))
        def _():
            with scope("rfirst"):
                reduce_first(i)

        relay_next(0, either(i == 0, tail_chip))
        relay_next(1, both(i == z.ns - 2, p < z.chips - 1))

        start_halo(both(beside, j == z.ns + 1), range(4))
        start_halo(both(slow, j == z.ns + 2), (0, 2, 3))
        send_forward(0, z.nb - PACK)

        @pl.when(both(first, tail_chip, j > z.ns, j < 2 * z.ns - 1))
        def _():
            with scope("middle"):
                make_middle(j)

        @pl.when(late)
        def _():
            with scope("hidden"):
                hidden_step(i)

        relay_next(1, either(i < z.ns - 2, tail_chip))

        @pl.when(both(first, tail_chip, either(j == 1, j == 2, j == z.ns - 1, j == z.ns, j == 2 * z.ns - 2)))
        def _():
            with scope("middle"):
                make_middle(jnp.where(j < 3, j - 1, jnp.where(late, j + j // (2 * z.ns - 2), j)))

        @pl.when(both(second, late))
        def _():
            with scope("rsecond"):
                reduce_second(i)

        send_forward(z.nb - PACK, z.nb)

        @pl.when(both(second, p < z.chips - 1, j == 2 * z.ns - 1))
        def _():
            with scope("handback"):
                hand_back(z.ns - 3)

        start_halo(both(border, j == 2 * z.ns - 1), (2, 3))

        @pl.when(both(jnp.logical_not(waits), j == z.ns - 1))
        def _():
            halo_tiles()

        @pl.when(both(second, j >= z.ns - 1, j < 2 * z.ns - 1))
        def _():
            base = (j + 1 - z.ns) * PACK

            @pl.when(j == z.ns - 1)
            def _():
                for k in range(PACK):
                    relay(base + k)

            with scope("partw"):
                for k in range(PACK):
                    mid_part(base + k, 1 - c).wait_recv()

    w_down = r.wb[:, :, 2].reshape(z.ng * 2 * UNIT, z.d)

    def finish(low, high):
        spots = [pl.ds(n, SMALL) for n in range(low, high, SMALL)]
        with scope("down"):
            outs = [mm(r.hid[at, :], w_down, NN) for at in spots]
            for at, out in zip(spots, outs):
                inverse = lax.rsqrt(jnp.mean(out * out, axis=-1, keepdims=True) + EPSILON)
                r.outs[at, :] = (r.att[at, :] + out * inverse * r.gains[...]).astype(BF)
        at = pl.ds(low, high - low)
        pltpu.make_async_copy(r.outs.at[at], r.mixed.at[at], r.store_sem.at[0]).start()

    finish(WINDOW, z.rows)

    @pl.when(waits)
    def _():
        halo_tiles()

    finish(0, WINDOW)

    with scope("tailfin"):
        @pl.when(first)
        def _():
            @pl.loop(0, z.nb)
            def _(g):
                @pl.when(tail_chip)
                def _():
                    r.ownm[g] = r.midq[g, z.chips - 1]

                @pl.when(jnp.logical_not(tail_chip))
                def _():
                    with scope("ownmw"):
                        own_mid(g, 0).wait_recv()

                with scope("owngw"):
                    own_grad(g, 0).wait_recv()
                with scope("fin"):
                    r.rows_out[g] = renormalize(r.ownm[g].astype(F32), r.og_r[g].astype(F32))
                    pltpu.make_async_copy(r.rows_out.at[g], r.final.at[:, g], r.rows_sem.at[0]).start()

        @pl.when(second)
        def _():
            @pl.loop(0, z.nb)
            def _(g):
                total, middle = split(r.gsum[g + z.nb]), split(r.wb[g + z.nb, c].astype(F32))
                mine, base = total[:, 0], middle[:, 0]
                for t in range(1, z.chips):
                    mine = jnp.where(p == t, total[:, t], mine)
                    base = jnp.where(p == t, middle[:, t], base)
                for t in range(z.chips):
                    @pl.when(p != t)
                    def _():
                        with scope("crossw"):
                            cross_grad(g, t, t).wait_recv()
                for t in range(z.chips):
                    mine = mine + jnp.where(p == t, 0.0, r.ox_r[g, t].astype(F32))
                with scope("fin"):
                    r.rows_out[g] = renormalize(base, mine)
                    pltpu.make_async_copy(r.rows_out.at[g], r.final.at[:, g], r.rows_sem.at[0]).start()

    with scope("tailsend"):
        @pl.when(s < z.count - 1)
        def _():
            for n in range(4):
                halo(n).wait_send()

        def sent(ref, sem):
            remote(ref, ref, sem.at[0], sem.at[0], s).wait_send()

        sent(r.pair_s, r.pair_ss)

        @pl.when(both(first, p < z.chips - 1))
        def _():
            sent(r.chain_s, r.chain_ss)

        @pl.when(both(second, p > 0))
        def _():
            sent(r.chain_s.at[pl.ds(0, z.nb)], r.chain_ss)

        @pl.when(either(both(first, tail_chip), both(second, p < z.chips - 1)))
        def _():
            sent(r.midb, r.mid_ss)

        @pl.when(second)
        def _():
            sent(r.midb, r.part_ss)
            sent(r.ox_s.at[:, pl.ds(0, z.chips - 1)], r.ox_ss)

        @pl.when(both(first, tail_chip))
        def _():
            sent(r.midq.at[:, pl.ds(0, z.chips - 1)], r.om_ss)

        @pl.when(both(second, head_chip))
        def _():
            sent(r.og_s, r.og_ss)

    with scope("tailstore"):
        pltpu.make_async_copy(r.outs, r.mixed, r.store_sem.at[0]).wait()
        pltpu.make_async_copy(r.rows_out, r.rows_out, r.rows_sem.at[0]).wait()


def hand_over_kernel(m_ref, f_ref, mo_ref, fo_ref, m_buf, f_buf, m_in, m_out, f_sem):
    step = m_buf.shape[0] // PIECES
    pieces = [pl.ds(n * step, step) for n in range(PIECES)]
    fetches = [pltpu.make_async_copy(m_ref.at[at], m_buf.at[at], m_in.at[n]) for n, at in enumerate(pieces)]
    stores = [pltpu.make_async_copy(m_buf.at[at], mo_ref.at[at], m_out.at[n]) for n, at in enumerate(pieces)]
    f_fetch = pltpu.make_async_copy(f_ref, f_buf, f_sem.at[0])
    f_store = pltpu.make_async_copy(f_buf, fo_ref, f_sem.at[1])
    f_fetch.start()
    for fetch in fetches:
        fetch.start()
    f_fetch.wait()
    f_store.start()
    for fetch, store in zip(fetches, stores):
        fetch.wait()
        store.start()
    f_store.wait()
    for store in stores:
        store.wait()


def hand_over(mixed, final):
    hbm = pl.BlockSpec(memory_space=pltpu.HBM)
    dma = pltpu.SemaphoreType.DMA
    return pl.pallas_call(
        hand_over_kernel,
        out_shape=tuple(jax.ShapeDtypeStruct(a.shape, a.dtype) for a in (mixed, final)),
        in_specs=[hbm] * 2,
        out_specs=(hbm,) * 2,
        scratch_shapes=[
            pltpu.VMEM(mixed.shape, mixed.dtype), pltpu.VMEM(final.shape, final.dtype),
            dma((PIECES,)), dma((PIECES,)), dma((2,)),
        ],
        compiler_params=pltpu.CompilerParams(vmem_limit_bytes=LIMIT),
    )(mixed, final)


def shards(
    attn_query, attn_key, attn_value, fast_query, fast_key, fast_value, rates, fast_weights, gain
):
    rows, d = fast_key.shape
    f = fast_weights.shape[1]
    z = sizes(lax.axis_size("seq"), rows, d, f, attn_query.shape[1])
    weights = jnp.swapaxes(fast_weights[0], 0, 1).reshape(3, 2, z.chips, 2, z.nb, z.rpo, d)
    parts = scratch(z)
    anywhere = pl.BlockSpec(memory_space=pl.ANY)
    hbm = pl.BlockSpec(memory_space=pltpu.HBM)
    vmem = pl.BlockSpec(memory_space=pltpu.VMEM)
    mixed, final = pl.pallas_call(
        functools.partial(kernel, z, INPUTS + ("mixed", "final") + tuple(parts)),
        out_shape=(
            jax.ShapeDtypeStruct((rows, d), BF),
            jax.ShapeDtypeStruct((3, z.nb, z.rpo, d), F32),
        ),
        in_specs=[hbm] * 9,
        out_specs=(anywhere, anywhere),
        scratch_shapes=list(parts.values()),
        compiler_params=pltpu.CompilerParams(
            vmem_limit_bytes=LIMIT, collective_id=0, has_side_effects=True
        ),
    )(
        attn_query, attn_key, attn_value, fast_query, fast_key, fast_value,
        rates.reshape(1, rows), weights, gain,
    )
    mixed, final = hand_over(mixed, final)
    return (mixed, jnp.swapaxes(final.reshape(3, z.share, d), 0, 1)[None])


def solution(mesh):
    tokens = P("seq", "head")
    in_specs = (tokens,) * 7 + (P("head", None, None, None), P("head", None))
    out_specs = (tokens, P("head", "seq", None, None))
    return jax.shard_map(shards, mesh=mesh, in_specs=in_specs, out_specs=out_specs, check_vma=False)
```

```python
import contextlib
import functools
import math
from types import SimpleNamespace

import jax
import jax.numpy as jnp
from jax import lax
from jax.experimental import pallas as pl
from jax.experimental.pallas import tpu as pltpu
from jax.sharding import PartitionSpec as P

AH = 128
WINDOW = 512
EPSILON = 1e-06
NEG = -1e30
NT = (((1,), (1,)), ((), ()))
NN = (((1,), (0,)), ((), ()))
LIMIT = 67043328
UNIT = 32
PACK = 2
TILE = 1024
SMALL = 512
TRACE = False
PIECES = 4
BF = jnp.bfloat16
F32 = jnp.float32


def scope(name):
    return jax.named_scope(name) if TRACE else contextlib.nullcontext()


def mm(a, b, dims):
    return lax.dot_general(a, b, dims, preferred_element_type=jnp.float32)


def sigmoid(v):
    return 0.5 * jnp.tanh(0.5 * v) + 0.5


def attend_scores(q, keys, biases):
    rows = q.shape[0]
    old, mid, new = (mm(q, k, NT) for k in keys)
    if biases[0] is not None:
        old = old + biases[0]
    if biases[1] is not None:
        mid = mid + biases[1]
    row = lax.broadcasted_iota(jnp.int32, (rows, rows), 0)
    col = lax.broadcasted_iota(jnp.int32, (rows, rows), 1)
    causal = col <= row
    return jnp.where(causal, new, old), mid, causal


def attend_values(edge, mid, causal, values):
    factor = math.log2(math.e) / math.sqrt(AH)
    top = jnp.max(jnp.maximum(edge, mid), -1, keepdims=True)
    edge = jnp.exp2((edge - top) * factor)
    mid = jnp.exp2((mid - top) * factor)
    p_new = jnp.where(causal, edge, 0.0).astype(BF)
    p_old = jnp.where(causal, 0.0, edge).astype(BF)
    ones = jnp.ones_like(values[0])
    values = jnp.concatenate([jnp.concatenate([v, ones], 1) for v in values], 0)
    out = mm(jnp.concatenate([p_old, mid.astype(BF), p_new], 1), values, NN)
    return out[:, :AH] * (1.0 / out[:, AH:])


def renormalize(previous, grad):
    moved = previous + grad
    return moved * (
        jnp.sqrt(jnp.mean(previous * previous, axis=-1, keepdims=True) + EPSILON)
        / jnp.sqrt(jnp.mean(moved * moved, axis=-1, keepdims=True) + EPSILON)
    )


def sizes(count, rows, d, f, columns):
    half = count // 2
    chips = half // 2
    rpo = UNIT // chips
    share = f // count
    per_block = share // rpo
    groups = 2 * per_block
    z = SimpleNamespace(
        count=count, half=half, chips=chips, rpo=rpo, share=share, nb=per_block, ng=groups,
        ns=groups // PACK, rows=rows, d=d, heads=columns // AH,
    )
    assert z.rpo * z.chips == UNIT and z.nb * z.rpo == z.share and z.ns * PACK == z.ng
    assert z.heads == z.ns and z.ng == 2 * z.ns and z.ns == 5 and z.rows == 2 * TILE
    return z


def scratch(z):
    unit = (3, UNIT, z.d)
    piece = (3, z.rpo, z.d)
    tokens = pltpu.VMEM((z.rows, z.d), BF)
    halo = pltpu.VMEM((WINDOW, z.d), BF)
    dma = pltpu.SemaphoreType.DMA
    return dict(
        qs=tokens, ks=tokens, vs=tokens, fqs=tokens, xs=tokens, ys=tokens, hid=tokens, outs=tokens,
        att=pltpu.VMEM((z.rows, z.d), F32),
        hk=halo, hv=halo,
        rates=pltpu.VMEM((1, z.rows), F32), gains=pltpu.VMEM((1, z.d), F32),
        wf=pltpu.VMEM((z.ng, 2, 3, z.chips, z.rpo, z.d), F32),
        wb=pltpu.VMEM((z.ng, 2) + unit, BF),
        acc=pltpu.VMEM((PACK, 2) + unit, F32),
        gsum=pltpu.VMEM((z.ng,) + unit, F32),
        pair_s=pltpu.VMEM((z.ng,) + unit, BF),
        pair_r=pltpu.VMEM((z.ng,) + unit, BF),
        chain_s=pltpu.VMEM((z.ng,) + unit, BF),
        chain_r=pltpu.VMEM((z.ng,) + unit, BF),
        midb=pltpu.VMEM((z.ng,) + unit, BF),
        midq=pltpu.VMEM((z.nb, z.chips) + piece, BF),
        ownm=pltpu.VMEM((z.nb,) + piece, BF),
        og_s=pltpu.VMEM((z.nb, z.chips) + piece, BF),
        ox_s=pltpu.VMEM((z.nb, z.chips) + piece, BF),
        og_r=pltpu.VMEM((z.nb,) + piece, BF),
        ox_r=pltpu.VMEM((z.nb, z.chips) + piece, BF),
        rows_out=pltpu.VMEM((z.nb, 3, z.rpo, z.d), F32), rows_sem=dma((1,)), load_sem=dma((10,)), store_sem=dma((1,)), wf_sem=dma((z.ns,)),
        halo_ss=dma((4,)), halo_rs=dma((4,)),
        pair_ss=dma((1,)), pair_rs=dma((z.ng,)),
        chain_ss=dma((1,)), chain_rs=dma((z.ng,)),
        mid_ss=dma((1,)), mid_rs=dma((z.ng,)),
        part_ss=dma((1,)), part_rs=dma((z.ng,)),
        om_ss=dma((1,)), om_rs=dma((z.nb,)),
        og_ss=dma((1,)), og_rs=dma((z.nb,)),
        ox_ss=dma((1,)), ox_rs=dma((z.nb, z.chips)),
    )


INPUTS = ("q", "k", "v", "fq", "fk", "fv", "rate", "w", "gain")


def kernel(z, names, *refs):
    r = SimpleNamespace(**dict(zip(names, refs)))
    s = lax.axis_index("seq")
    hd = lax.axis_index("head")
    chip = lax.div(s, 2)
    c = s - 2 * chip
    b = lax.div(chip, z.chips)
    p = chip - b * z.chips
    first, second = b == 0, b == 1
    head_chip, tail_chip = p == 0, p == z.chips - 1

    def both(*conditions):
        return functools.reduce(jnp.logical_and, conditions)

    def either(*conditions):
        return functools.reduce(jnp.logical_or, conditions)

    def remote(src, dst, ss, rs, device):
        return pltpu.make_async_remote_copy(
            src_ref=src, dst_ref=dst, send_sem=ss, recv_sem=rs,
            device_id=(device, hd), device_id_type=pl.DeviceIdType.MESH,
        )

    def pair(g):
        return remote(r.pair_s.at[g], r.pair_r.at[g], r.pair_ss.at[0], r.pair_rs.at[g], s + 1 - 2 * c)

    def chain(g):
        return remote(r.chain_s.at[g], r.chain_r.at[g], r.chain_ss.at[0], r.chain_rs.at[g], s + 2 - 4 * b)

    def mid_out(g):
        return remote(r.midb.at[g], r.wb.at[g, c], r.mid_ss.at[0], r.mid_rs.at[g], s + 2)

    def mid_on(g):
        return remote(r.wb.at[g, c], r.wb.at[g, c], r.mid_ss.at[0], r.mid_rs.at[g], s + 2)

    def mid_part(g, core):
        return remote(r.wb.at[g, core], r.wb.at[g, core], r.part_ss.at[0], r.part_rs.at[g], s + 1 - 2 * c)

    def own_mid(g, t):
        return remote(r.midq.at[g, t], r.ownm.at[g], r.om_ss.at[0], r.om_rs.at[g], 2 * t + c)

    def own_grad(g, t):
        return remote(r.og_s.at[g, t], r.og_r.at[g], r.og_ss.at[0], r.og_rs.at[g], 2 * t + c)

    def cross_grad(g, t, origin):
        return remote(
            r.ox_s.at[g, t], r.ox_r.at[g, origin], r.ox_ss.at[0], r.ox_rs.at[g, origin],
            z.half + 2 * t + c,
        )

    def halo(n):
        src, dst = ((r.k, r.hk), (r.v, r.hv))[n // 2]
        half = WINDOW // 2
        start = n % 2 * half
        return remote(
            src.at[pl.ds(z.rows - WINDOW + start, half)], dst.at[pl.ds(start, half)],
            r.halo_ss.at[n], r.halo_rs.at[n], s + 1,
        )

    def load(n):
        src, dst = (
            (r.q, r.qs), (r.k, r.ks), (r.v, r.vs), (r.fq, r.fqs), (r.rate, r.rates), (r.gain, r.gains),
        )[n]
        return pltpu.make_async_copy(src, dst, r.load_sem.at[n + n // 4 * 2])

    def load_rows(n, half):
        src, dst = ((r.fk, r.xs), (r.fv, r.ys))[n]
        at = pl.ds(half * TILE, TILE)
        return pltpu.make_async_copy(src.at[at], dst.at[at], r.load_sem.at[4 + n + 4 * half])

    def load_w(g, core):
        block = lax.div(g, z.nb)
        return pltpu.make_async_copy(
            r.w.at[:, block, :, core, g - block * z.nb], r.wf.at[g, core], r.wf_sem.at[lax.div(g, PACK)]
        )

    def peer(n):
        other, core, block = n // 2, n % 2, n // z.half
        near = b == block
        if other < z.chips:
            near = either(near, chip == z.chips)
        if other == z.chips:
            near = either(near, first)
        return both(s != n, either(both(c == core, near), s == n - 1, s == n + 1))

    barrier = pltpu.get_barrier_semaphore()
    for n in range(z.count):
        @pl.when(peer(n))
        def _():
            pl.semaphore_signal(
                barrier, inc=1, device_id=(n, hd), device_id_type=pl.DeviceIdType.MESH
            )

    def load_weights(low, high):
        @pl.loop(low, high)
        def _(g):
            for core in range(2):
                load_w(g, core).start()

    @pl.when(first)
    def _():
        load_weights(0, PACK)
        load(4).start()
        for half in range(2):
            for n in range(2):
                load_rows(n, half).start()

    @pl.when(second)
    def _():
        for n in (1, 0, 2, 4):
            load(n).start()

    load(5).start()

    @pl.when(s == 0)
    def _():
        r.hk[...] = jnp.zeros_like(r.hk)
        r.hv[...] = jnp.zeros_like(r.hv)

    sends = s < z.count - 1
    border = both(first, c == 1, tail_chip)
    slow = both(first, c == 1, p < z.chips - 1)
    beside = both(first, c == 0)

    def start_halo(condition, parts):
        @pl.when(both(sends, condition))
        def _():
            for n in parts:
                halo(n).start()

    def enter():
        pl.semaphore_wait(barrier, sum(jnp.where(peer(n), 1, 0) for n in range(z.count)))

        start_halo(second, range(4))
        start_halo(border, (0, 1))
        start_halo(slow, (1,))

        load(5).wait()

    def load_rest():
        @pl.when(first)
        def _():
            for n in (0, 1, 2, 3):
                load(n).start()

        @pl.when(second)
        def _():
            for half in range(2):
                for n in range(2):
                    load_rows(n, half).start()
            load(3).start()

    def weights(i):
        w = r.wb[pl.ds(i * PACK, PACK)].reshape(PACK * 2, 3, UNIT, z.d)
        return w

    def grad_step(i, between):
        n = PACK * 2
        w = weights(i)
        w_gu = w[:, 0:2].reshape(n * 2 * UNIT, z.d)
        w_down = w[:, 2].reshape(n * UNIT, z.d)
        tiles = z.rows // TILE

        def rows(ref, t):
            return ref[t * TILE : (t + 1) * TILE, :]

        def products(t):
            return mm(w_gu, rows(r.xs, t), NT), mm(w_down, rows(r.ys, t), NT)

        for t in range(tiles):
            if t == 1:
                between()
            gu, back = products(t)
            rate = r.rates[:, t * TILE : (t + 1) * TILE]
            gu = gu.reshape(n, 2, UNIT, TILE)
            back = back * rate
            gate = gu[:, 0].reshape(n * UNIT, TILE)
            up = gu[:, 1].reshape(n * UNIT, TILE)
            sg = sigmoid(gate)
            active = gate * sg
            hidden = (active * up * rate).astype(BF)
            up_grad = (back * active).astype(BF)
            gate_grad = (back * up * (sg * (1.0 + gate * (1.0 - sg)))).astype(BF)
            both_grad = jnp.concatenate(
                [gate_grad.reshape(n, 1, UNIT, TILE), up_grad.reshape(n, 1, UNIT, TILE)], 1
            ).reshape(n * 2 * UNIT, TILE)
            wide = mm(both_grad, rows(r.xs, t), NN).reshape(PACK, 2, 2, UNIT, z.d)
            down = mm(hidden, rows(r.ys, t), NN).reshape(PACK, 2, UNIT, z.d)
            if t == 0:
                r.acc[:, :, 0:2] = wide
                r.acc[:, :, 2] = down
            else:
                r.acc[:, :, 0:2] += wide
                r.acc[:, :, 2] += down
        for k in range(PACK):
            g = i * PACK + k
            r.gsum[g] = r.acc[k, c]
            r.pair_s[g] = r.acc[k, 1 - c].astype(BF)

    def combine(g):
        pair(g).wait_recv()
        r.gsum[g] += r.pair_r[g].astype(F32)

    def add_chain(g):
        chain(g).wait_recv()
        r.gsum[g] += r.chain_r[g].astype(F32)

    def send_chain(g):
        r.chain_s[g] = r.gsum[g].astype(BF)
        chain(g).start()

    def split(unit):
        return unit.reshape(3, z.chips, z.rpo, z.d)

    def reduce_first(i):
        for k in range(PACK):
            g = i * PACK + k
            combine(g)

            @pl.when(p > 0)
            def _():
                add_chain(g)

            send_chain(g)

    def make_middle(g):
        combine(g)
        add_chain(g)
        middle = renormalize(r.wf[g, c].reshape(3, UNIT, z.d), r.gsum[g])
        r.midb[g] = middle.astype(BF)
        mid_out(g).start()

        @pl.when(g < z.nb)
        def _():
            pieces = split(middle)
            for t in range(z.chips):
                r.midq[g, t] = pieces[:, t].astype(BF)
                if t < z.chips - 1:
                    own_mid(g, t).start()

    def relay(g):
        mid_on(g).wait_recv()

        @pl.when(p < z.chips - 1)
        def _():
            mid_on(g).start()

        mid_part(g, c).start()

    def reduce_second(i):
        for k in range(PACK):
            g = i * PACK + k
            combine(g)

            @pl.when(both(g < z.nb, tail_chip))
            def _():
                send_chain(g)

            @pl.when(g >= z.nb)
            def _():
                pieces = split(r.gsum[g])
                for t in range(z.chips):
                    @pl.when(p != t)
                    def _():
                        r.ox_s[g - z.nb, t] = pieces[:, t].astype(BF)

                    @pl.when(p > t)
                    def _():
                        cross_grad(g - z.nb, t, p).start()

    def hand_back(i):
        for k in range(PACK):
            g = i * PACK + k

            @pl.when(g < z.nb)
            def _():
                add_chain(g)

                @pl.when(p > 0)
                def _():
                    send_chain(g)

                @pl.when(head_chip)
                def _():
                    pieces = split(r.gsum[g])
                    for t in range(z.chips):
                        r.og_s[g, t] = pieces[:, t].astype(BF)
                        own_grad(g, t).start()

    tile = WINDOW // 2

    def attention_tiles(h, tiles, bias):
        columns = pl.ds(pl.multiple_of(h * AH, AH), AH)

        def block(ref, halo_ref, at):
            if at < 0:
                return halo_ref[(at + 2) * tile : (at + 3) * tile, columns]
            return ref[at * tile : (at + 1) * tile, columns]

        def scores(t):
            keys = [block(r.ks, r.hk, t - 2 + n) for n in range(3)]
            biases = [bias if t - 2 + n < 0 else None for n in range(2)]
            return attend_scores(r.qs[t * tile : (t + 1) * tile, columns], keys, biases)

        ahead = scores(tiles[0])
        for n, t in enumerate(tiles):
            now = ahead
            if n + 1 < len(tiles):
                ahead = scores(tiles[n + 1])
            values = [block(r.vs, r.hv, t - 2 + m) for m in range(3)]
            r.att[t * tile : (t + 1) * tile, columns] = attend_values(*now, values)

    def hidden_step(i):
        n = PACK * 2 * UNIT
        w = weights(i)
        w_gu = jnp.concatenate([w[:, 0].reshape(n, z.d), w[:, 1].reshape(n, z.d)], 0)
        columns = pl.ds(pl.multiple_of(i * n, n), n)
        tiles = z.rows // SMALL

        def products(t):
            return mm(r.fqs[t * SMALL : (t + 1) * SMALL, :], w_gu, NT)

        ahead = products(0)
        for t in range(tiles):
            now = ahead
            if t + 1 < tiles:
                ahead = products(t + 1)
            gate, up = now[:, :n], now[:, n:]
            r.hid[t * SMALL : (t + 1) * SMALL, columns] = (gate * sigmoid(gate) * up).astype(BF)

    waits = either(first, s == z.half)

    def halo_tiles():
        @pl.when(s > 0)
        def _():
            with scope("halow"):
                for n in range(4):
                    halo(n).wait_recv()

        bias = jnp.where(s == 0, jnp.float32(NEG), jnp.float32(0.0))

        @pl.loop(0, z.heads)
        def _(h):
            with scope("atth"):
                attention_tiles(h, range(2), bias)

    @pl.loop(0, 2 * z.ns)
    def _(j):
        early, late = j < z.ns, j >= z.ns
        i = lax.rem(j, z.ns)

        @pl.when(either(both(first, j == 0), both(second, j == z.ns)))
        def _():
            load(4).wait()
            for n in range(2):
                load_rows(n, 0).wait()

        @pl.when(either(both(second, j == 0), both(first, j == z.ns)))
        def _():
            for n in (0, 1, 2):
                load(n).wait()

        @pl.when(j == z.ns)
        def _():
            load(3).wait()

        @pl.when(both(second, j == 0))
        def _():
            with scope("enter"):
                enter()

        @pl.when(both(first, early))
        def _():
            step = r.wf.at[pl.ds(i * PACK, PACK)]
            pltpu.make_async_copy(step, step, r.wf_sem.at[i]).wait()
            for k in range(PACK):
                g = i * PACK + k
                for core in range(2):
                    r.wb[g, core] = r.wf[g, core].reshape(3, UNIT, z.d).astype(BF)

            @pl.when(j == 0)
            def _():
                load_weights(PACK, z.ng)

        @pl.when(j == 1)
        def _():
            load_rest()

        differentiate = first == early

        def relay_next(k, ready):
            @pl.when(both(second, late, j < 2 * z.ns - 1, ready))
            def _():
                with scope("relay%d" % k):
                    relay((i + 1) * PACK + k)

        def between():
            @pl.when(either(both(first, j == 0), both(second, j == z.ns)))
            def _():
                for n in range(2):
                    load_rows(n, 1).wait()

            @pl.when(both(first, j == 0))
            def _():
                with scope("enter"):
                    enter()

            relay_next(0, i > 0)

            @pl.when(both(second, p < z.chips - 1, j >= z.ns + 3))
            def _():
                with scope("handback"):
                    hand_back(j - z.ns - 3)

            @pl.when(both(first, tail_chip, either(j == z.ns - 2, j == z.ns - 1)))
            def _():
                with scope("middle"):
                    make_middle(j - 1)

        def send_forward(low, high):
            @pl.when(both(second, j == 2 * z.ns - 1))
            def _():
                for t in range(1, z.chips):
                    @pl.when(p < t)
                    def _():
                        @pl.loop(low, high)
                        def _(g):
                            cross_grad(g, t, p).start()

        @pl.when(differentiate)
        def _():
            with scope("grad"):
                grad_step(i, between)

        @pl.when(jnp.logical_not(differentiate))
        def _():
            with scope("att"):
                attention_tiles(i, range(2, z.rows // tile), None)

        @pl.when(differentiate)
        def _():
            for k in range(PACK):
                pair(i * PACK + k).start()

        @pl.when(both(first, p < z.chips - 1, early))
        def _():
            with scope("rfirst"):
                reduce_first(i)

        relay_next(0, i == 0)
        relay_next(1, either(i == z.ns - 2, both(tail_chip, i > 0)))

        start_halo(both(beside, j == z.ns + 1), range(4))
        start_halo(both(slow, j == z.ns + 2), (0, 2, 3))
        send_forward(0, z.nb - PACK)

        @pl.when(both(first, tail_chip, j > z.ns, j < 2 * z.ns - 1))
        def _():
            with scope("middle"):
                make_middle(j)

        @pl.when(late)
        def _():
            with scope("hidden"):
                hidden_step(i)

        relay_next(1, both(i < z.ns - 2, either(i == 0, p < z.chips - 1)))

        @pl.when(both(first, tail_chip, either(j == 1, j == 2, j == z.ns - 1, j == z.ns, j == 2 * z.ns - 2)))
        def _():
            with scope("middle"):
                make_middle(jnp.where(j < 3, j - 1, jnp.where(late, j + j // (2 * z.ns - 2), j)))

        @pl.when(both(second, late))
        def _():
            with scope("rsecond"):
                reduce_second(i)

        send_forward(z.nb - PACK, z.nb)

        @pl.when(both(second, p < z.chips - 1, j == 2 * z.ns - 1))
        def _():
            with scope("handback"):
                hand_back(z.ns - 3)

        start_halo(both(border, j == 2 * z.ns - 1), (2, 3))

        @pl.when(both(jnp.logical_not(waits), j == z.ns - 1))
        def _():
            halo_tiles()

        @pl.when(both(second, j >= z.ns - 1, j < 2 * z.ns - 1))
        def _():
            base = (j + 1 - z.ns) * PACK

            @pl.when(j == z.ns - 1)
            def _():
                for k in range(PACK):
                    relay(base + k)

            with scope("partw"):
                for k in range(PACK):
                    mid_part(base + k, 1 - c).wait_recv()

    w_down = r.wb[:, :, 2].reshape(z.ng * 2 * UNIT, z.d)

    def finish(low, high):
        spots = [pl.ds(n, SMALL) for n in range(low, high, SMALL)]
        with scope("down"):
            outs = [mm(r.hid[at, :], w_down, NN) for at in spots]
            for at, out in zip(spots, outs):
                inverse = lax.rsqrt(jnp.mean(out * out, axis=-1, keepdims=True) + EPSILON)
                r.outs[at, :] = (r.att[at, :] + out * inverse * r.gains[...]).astype(BF)
        at = pl.ds(low, high - low)
        pltpu.make_async_copy(r.outs.at[at], r.mixed.at[at], r.store_sem.at[0]).start()

    finish(WINDOW, z.rows)

    @pl.when(waits)
    def _():
        halo_tiles()

    finish(0, WINDOW)

    with scope("tailfin"):
        @pl.when(first)
        def _():
            @pl.loop(0, z.nb)
            def _(g):
                @pl.when(tail_chip)
                def _():
                    r.ownm[g] = r.midq[g, z.chips - 1]

                @pl.when(jnp.logical_not(tail_chip))
                def _():
                    with scope("ownmw"):
                        own_mid(g, 0).wait_recv()

                with scope("owngw"):
                    own_grad(g, 0).wait_recv()
                with scope("fin"):
                    r.rows_out[g] = renormalize(r.ownm[g].astype(F32), r.og_r[g].astype(F32))
                    pltpu.make_async_copy(r.rows_out.at[g], r.final.at[:, g], r.rows_sem.at[0]).start()

        @pl.when(second)
        def _():
            @pl.loop(0, z.nb)
            def _(g):
                total, middle = split(r.gsum[g + z.nb]), split(r.wb[g + z.nb, c].astype(F32))
                mine, base = total[:, 0], middle[:, 0]
                for t in range(1, z.chips):
                    mine = jnp.where(p == t, total[:, t], mine)
                    base = jnp.where(p == t, middle[:, t], base)
                for t in range(z.chips):
                    @pl.when(p != t)
                    def _():
                        with scope("crossw"):
                            cross_grad(g, t, t).wait_recv()
                for t in range(z.chips):
                    mine = mine + jnp.where(p == t, 0.0, r.ox_r[g, t].astype(F32))
                with scope("fin"):
                    r.rows_out[g] = renormalize(base, mine)
                    pltpu.make_async_copy(r.rows_out.at[g], r.final.at[:, g], r.rows_sem.at[0]).start()

    with scope("tailsend"):
        @pl.when(s < z.count - 1)
        def _():
            for n in range(4):
                halo(n).wait_send()

        def sent(ref, sem):
            remote(ref, ref, sem.at[0], sem.at[0], s).wait_send()

        sent(r.pair_s, r.pair_ss)

        @pl.when(both(first, p < z.chips - 1))
        def _():
            sent(r.chain_s, r.chain_ss)

        @pl.when(both(second, p > 0))
        def _():
            sent(r.chain_s.at[pl.ds(0, z.nb)], r.chain_ss)

        @pl.when(either(both(first, tail_chip), both(second, p < z.chips - 1)))
        def _():
            sent(r.midb, r.mid_ss)

        @pl.when(second)
        def _():
            sent(r.midb, r.part_ss)
            sent(r.ox_s.at[:, pl.ds(0, z.chips - 1)], r.ox_ss)

        @pl.when(both(first, tail_chip))
        def _():
            sent(r.midq.at[:, pl.ds(0, z.chips - 1)], r.om_ss)

        @pl.when(both(second, head_chip))
        def _():
            sent(r.og_s, r.og_ss)

    with scope("tailstore"):
        pltpu.make_async_copy(r.outs, r.mixed, r.store_sem.at[0]).wait()
        pltpu.make_async_copy(r.rows_out, r.rows_out, r.rows_sem.at[0]).wait()


def hand_over_kernel(m_ref, f_ref, mo_ref, fo_ref, m_buf, f_buf, m_in, m_out, f_sem):
    step = m_buf.shape[0] // PIECES
    pieces = [pl.ds(n * step, step) for n in range(PIECES)]
    fetches = [pltpu.make_async_copy(m_ref.at[at], m_buf.at[at], m_in.at[n]) for n, at in enumerate(pieces)]
    stores = [pltpu.make_async_copy(m_buf.at[at], mo_ref.at[at], m_out.at[n]) for n, at in enumerate(pieces)]
    f_fetch = pltpu.make_async_copy(f_ref, f_buf, f_sem.at[0])
    f_store = pltpu.make_async_copy(f_buf, fo_ref, f_sem.at[1])
    f_fetch.start()
    for fetch in fetches:
        fetch.start()
    f_fetch.wait()
    f_store.start()
    for fetch, store in zip(fetches, stores):
        fetch.wait()
        store.start()
    f_store.wait()
    for store in stores:
        store.wait()


def hand_over(mixed, final):
    hbm = pl.BlockSpec(memory_space=pltpu.HBM)
    dma = pltpu.SemaphoreType.DMA
    return pl.pallas_call(
        hand_over_kernel,
        out_shape=tuple(jax.ShapeDtypeStruct(a.shape, a.dtype) for a in (mixed, final)),
        in_specs=[hbm] * 2,
        out_specs=(hbm,) * 2,
        scratch_shapes=[
            pltpu.VMEM(mixed.shape, mixed.dtype), pltpu.VMEM(final.shape, final.dtype),
            dma((PIECES,)), dma((PIECES,)), dma((2,)),
        ],
        compiler_params=pltpu.CompilerParams(vmem_limit_bytes=LIMIT),
    )(mixed, final)


def shards(
    attn_query, attn_key, attn_value, fast_query, fast_key, fast_value, rates, fast_weights, gain
):
    rows, d = fast_key.shape
    f = fast_weights.shape[1]
    z = sizes(lax.axis_size("seq"), rows, d, f, attn_query.shape[1])
    weights = jnp.swapaxes(fast_weights[0], 0, 1).reshape(3, 2, z.chips, 2, z.nb, z.rpo, d)
    parts = scratch(z)
    anywhere = pl.BlockSpec(memory_space=pl.ANY)
    hbm = pl.BlockSpec(memory_space=pltpu.HBM)
    vmem = pl.BlockSpec(memory_space=pltpu.VMEM)
    mixed, final = pl.pallas_call(
        functools.partial(kernel, z, INPUTS + ("mixed", "final") + tuple(parts)),
        out_shape=(
            jax.ShapeDtypeStruct((rows, d), BF),
            jax.ShapeDtypeStruct((3, z.nb, z.rpo, d), F32),
        ),
        in_specs=[hbm] * 9,
        out_specs=(anywhere, anywhere),
        scratch_shapes=list(parts.values()),
        compiler_params=pltpu.CompilerParams(
            vmem_limit_bytes=LIMIT, collective_id=0, has_side_effects=True
        ),
    )(
        attn_query, attn_key, attn_value, fast_query, fast_key, fast_value,
        rates.reshape(1, rows), weights, gain,
    )
    mixed, final = hand_over(mixed, final)
    return (mixed, jnp.swapaxes(final.reshape(3, z.share, d), 0, 1)[None])


def solution(mesh):
    tokens = P("seq", "head")
    in_specs = (tokens,) * 7 + (P("head", None, None, None), P("head", None))
    out_specs = (tokens, P("head", "seq", None, None))
    return jax.shard_map(shards, mesh=mesh, in_specs=in_specs, out_specs=out_specs, check_vma=False)
```

```python
import contextlib
import functools
import math
from types import SimpleNamespace

import jax
import jax.numpy as jnp
from jax import lax
from jax.experimental import pallas as pl
from jax.experimental.pallas import tpu as pltpu
from jax.sharding import PartitionSpec as P

AH = 128
WINDOW = 512
EPSILON = 1e-06
NEG = -1e30
NT = (((1,), (1,)), ((), ()))
NN = (((1,), (0,)), ((), ()))
LIMIT = 67043328
UNIT = 32
PACK = 2
TILE = 1024
SMALL = 512
TRACE = False
PIECES = 2
BF = jnp.bfloat16
F32 = jnp.float32


def scope(name):
    return jax.named_scope(name) if TRACE else contextlib.nullcontext()


def mm(a, b, dims):
    return lax.dot_general(a, b, dims, preferred_element_type=jnp.float32)


def sigmoid(v):
    return 0.5 * jnp.tanh(0.5 * v) + 0.5


def attend_scores(q, keys, biases):
    rows = q.shape[0]
    old, mid, new = (mm(q, k, NT) for k in keys)
    if biases[0] is not None:
        old = old + biases[0]
    if biases[1] is not None:
        mid = mid + biases[1]
    row = lax.broadcasted_iota(jnp.int32, (rows, rows), 0)
    col = lax.broadcasted_iota(jnp.int32, (rows, rows), 1)
    causal = col <= row
    return jnp.where(causal, new, old), mid, causal


def attend_values(edge, mid, causal, values):
    factor = math.log2(math.e) / math.sqrt(AH)
    top = jnp.max(jnp.maximum(edge, mid), -1, keepdims=True)
    edge = jnp.exp2((edge - top) * factor)
    mid = jnp.exp2((mid - top) * factor)
    p_new = jnp.where(causal, edge, 0.0).astype(BF)
    p_old = jnp.where(causal, 0.0, edge).astype(BF)
    ones = jnp.ones_like(values[0])
    values = jnp.concatenate([jnp.concatenate([v, ones], 1) for v in values], 0)
    out = mm(jnp.concatenate([p_old, mid.astype(BF), p_new], 1), values, NN)
    return out[:, :AH] * (1.0 / out[:, AH:])


def renormalize(previous, grad):
    moved = previous + grad
    return moved * (
        jnp.sqrt(jnp.mean(previous * previous, axis=-1, keepdims=True) + EPSILON)
        / jnp.sqrt(jnp.mean(moved * moved, axis=-1, keepdims=True) + EPSILON)
    )


def sizes(count, rows, d, f, columns):
    half = count // 2
    chips = half // 2
    rpo = UNIT // chips
    share = f // count
    per_block = share // rpo
    groups = 2 * per_block
    z = SimpleNamespace(
        count=count, half=half, chips=chips, rpo=rpo, share=share, nb=per_block, ng=groups,
        ns=groups // PACK, rows=rows, d=d, heads=columns // AH,
    )
    assert z.rpo * z.chips == UNIT and z.nb * z.rpo == z.share and z.ns * PACK == z.ng
    assert z.heads == z.ns and z.ng == 2 * z.ns and z.ns == 5 and z.rows == 2 * TILE
    return z


def scratch(z):
    unit = (3, UNIT, z.d)
    piece = (3, z.rpo, z.d)
    tokens = pltpu.VMEM((z.rows, z.d), BF)
    halo = pltpu.VMEM((WINDOW, z.d), BF)
    dma = pltpu.SemaphoreType.DMA
    return dict(
        qs=tokens, ks=tokens, vs=tokens, fqs=tokens, xs=tokens, ys=tokens, hid=tokens, outs=tokens,
        att=pltpu.VMEM((z.rows, z.d), F32),
        hk=halo, hv=halo,
        rates=pltpu.VMEM((1, z.rows), F32), gains=pltpu.VMEM((1, z.d), F32),
        wf=pltpu.VMEM((z.ng, 2, 3, z.chips, z.rpo, z.d), F32),
        wb=pltpu.VMEM((z.ng, 2) + unit, BF),
        acc=pltpu.VMEM((PACK, 2) + unit, F32),
        gsum=pltpu.VMEM((z.ng,) + unit, F32),
        pair_s=pltpu.VMEM((z.ng,) + unit, BF),
        pair_r=pltpu.VMEM((z.ng,) + unit, BF),
        chain_s=pltpu.VMEM((z.ng,) + unit, BF),
        chain_r=pltpu.VMEM((z.ng,) + unit, BF),
        midb=pltpu.VMEM((z.ng,) + unit, BF),
        midq=pltpu.VMEM((z.nb, z.chips) + piece, BF),
        ownm=pltpu.VMEM((z.nb,) + piece, BF),
        og_s=pltpu.VMEM((z.nb, z.chips) + piece, BF),
        ox_s=pltpu.VMEM((z.nb, z.chips) + piece, BF),
        og_r=pltpu.VMEM((z.nb,) + piece, BF),
        ox_r=pltpu.VMEM((z.nb, z.chips) + piece, BF),
        rows_out=pltpu.VMEM((z.nb, 3, z.rpo, z.d), F32), rows_sem=dma((1,)), load_sem=dma((10,)), store_sem=dma((1,)), wf_sem=dma((z.ns,)),
        halo_ss=dma((4,)), halo_rs=dma((4,)),
        pair_ss=dma((1,)), pair_rs=dma((z.ng,)),
        chain_ss=dma((1,)), chain_rs=dma((z.ng,)),
        mid_ss=dma((1,)), mid_rs=dma((z.ng,)),
        part_ss=dma((1,)), part_rs=dma((z.ng,)),
        om_ss=dma((1,)), om_rs=dma((z.nb,)),
        og_ss=dma((1,)), og_rs=dma((z.nb,)),
        ox_ss=dma((1,)), ox_rs=dma((z.nb, z.chips)),
    )


INPUTS = ("q", "k", "v", "fq", "fk", "fv", "rate", "w", "gain")


def kernel(z, names, *refs):
    r = SimpleNamespace(**dict(zip(names, refs)))
    s = lax.axis_index("seq")
    hd = lax.axis_index("head")
    chip = lax.div(s, 2)
    c = s - 2 * chip
    b = lax.div(chip, z.chips)
    p = chip - b * z.chips
    first, second = b == 0, b == 1
    head_chip, tail_chip = p == 0, p == z.chips - 1

    def both(*conditions):
        return functools.reduce(jnp.logical_and, conditions)

    def either(*conditions):
        return functools.reduce(jnp.logical_or, conditions)

    def remote(src, dst, ss, rs, device):
        return pltpu.make_async_remote_copy(
            src_ref=src, dst_ref=dst, send_sem=ss, recv_sem=rs,
            device_id=(device, hd), device_id_type=pl.DeviceIdType.MESH,
        )

    def pair(g):
        return remote(r.pair_s.at[g], r.pair_r.at[g], r.pair_ss.at[0], r.pair_rs.at[g], s + 1 - 2 * c)

    def chain(g):
        return remote(r.chain_s.at[g], r.chain_r.at[g], r.chain_ss.at[0], r.chain_rs.at[g], s + 2 - 4 * b)

    def mid_out(g):
        return remote(r.midb.at[g], r.wb.at[g, c], r.mid_ss.at[0], r.mid_rs.at[g], s + 2)

    def mid_on(g):
        return remote(r.wb.at[g, c], r.wb.at[g, c], r.mid_ss.at[0], r.mid_rs.at[g], s + 2)

    def mid_part(g, core):
        return remote(r.wb.at[g, core], r.wb.at[g, core], r.part_ss.at[0], r.part_rs.at[g], s + 1 - 2 * c)

    def own_mid(g, t):
        return remote(r.midq.at[g, t], r.ownm.at[g], r.om_ss.at[0], r.om_rs.at[g], 2 * t + c)

    def own_grad(g, t):
        return remote(r.og_s.at[g, t], r.og_r.at[g], r.og_ss.at[0], r.og_rs.at[g], 2 * t + c)

    def cross_grad(g, t, origin):
        return remote(
            r.ox_s.at[g, t], r.ox_r.at[g, origin], r.ox_ss.at[0], r.ox_rs.at[g, origin],
            z.half + 2 * t + c,
        )

    def halo(n):
        src, dst = ((r.k, r.hk), (r.v, r.hv))[n // 2]
        half = WINDOW // 2
        start = n % 2 * half
        return remote(
            src.at[pl.ds(z.rows - WINDOW + start, half)], dst.at[pl.ds(start, half)],
            r.halo_ss.at[n], r.halo_rs.at[n], s + 1,
        )

    def load(n):
        src, dst = (
            (r.q, r.qs), (r.k, r.ks), (r.v, r.vs), (r.fq, r.fqs), (r.rate, r.rates), (r.gain, r.gains),
        )[n]
        return pltpu.make_async_copy(src, dst, r.load_sem.at[n + n // 4 * 2])

    def load_rows(n, half):
        src, dst = ((r.fk, r.xs), (r.fv, r.ys))[n]
        at = pl.ds(half * TILE, TILE)
        return pltpu.make_async_copy(src.at[at], dst.at[at], r.load_sem.at[4 + n + 4 * half])

    def load_w(g, core):
        block = lax.div(g, z.nb)
        return pltpu.make_async_copy(
            r.w.at[:, block, :, core, g - block * z.nb], r.wf.at[g, core], r.wf_sem.at[lax.div(g, PACK)]
        )

    def peer(n):
        other, core, block = n // 2, n % 2, n // z.half
        near = b == block
        if other < z.chips:
            near = either(near, chip == z.chips)
        if other == z.chips:
            near = either(near, first)
        return both(s != n, either(both(c == core, near), s == n - 1, s == n + 1))

    barrier = pltpu.get_barrier_semaphore()
    for n in range(z.count):
        @pl.when(peer(n))
        def _():
            pl.semaphore_signal(
                barrier, inc=1, device_id=(n, hd), device_id_type=pl.DeviceIdType.MESH
            )

    def load_weights(low, high):
        @pl.loop(low, high)
        def _(g):
            for core in range(2):
                load_w(g, core).start()

    @pl.when(first)
    def _():
        load_weights(0, PACK)
        load(4).start()
        for half in range(2):
            for n in range(2):
                load_rows(n, half).start()

    @pl.when(second)
    def _():
        for n in (1, 0, 2, 4):
            load(n).start()

    load(5).start()

    @pl.when(s == 0)
    def _():
        r.hk[...] = jnp.zeros_like(r.hk)
        r.hv[...] = jnp.zeros_like(r.hv)

    sends = s < z.count - 1
    border = both(first, c == 1, tail_chip)
    slow = both(first, c == 1, p < z.chips - 1)
    beside = both(first, c == 0)

    def start_halo(condition, parts):
        @pl.when(both(sends, condition))
        def _():
            for n in parts:
                halo(n).start()

    def enter():
        pl.semaphore_wait(barrier, sum(jnp.where(peer(n), 1, 0) for n in range(z.count)))

        start_halo(second, range(4))
        start_halo(border, (0, 1))
        start_halo(slow, (1,))

        load(5).wait()

    def load_rest():
        @pl.when(first)
        def _():
            for n in (0, 1, 2, 3):
                load(n).start()

        @pl.when(second)
        def _():
            for half in range(2):
                for n in range(2):
                    load_rows(n, half).start()
            load(3).start()

    def weights(i):
        w = r.wb[pl.ds(i * PACK, PACK)].reshape(PACK * 2, 3, UNIT, z.d)
        return w

    def grad_step(i, between):
        n = PACK * 2
        w = weights(i)
        w_gu = w[:, 0:2].reshape(n * 2 * UNIT, z.d)
        w_down = w[:, 2].reshape(n * UNIT, z.d)
        tiles = z.rows // TILE

        def rows(ref, t):
            return ref[t * TILE : (t + 1) * TILE, :]

        def products(t):
            return mm(w_gu, rows(r.xs, t), NT), mm(w_down, rows(r.ys, t), NT)

        for t in range(tiles):
            if t == 1:
                between()
            gu, back = products(t)
            rate = r.rates[:, t * TILE : (t + 1) * TILE]
            gu = gu.reshape(n, 2, UNIT, TILE)
            back = back * rate
            gate = gu[:, 0].reshape(n * UNIT, TILE)
            up = gu[:, 1].reshape(n * UNIT, TILE)
            sg = sigmoid(gate)
            active = gate * sg
            hidden = (active * up * rate).astype(BF)
            up_grad = (back * active).astype(BF)
            gate_grad = (back * up * (sg * (1.0 + gate * (1.0 - sg)))).astype(BF)
            both_grad = jnp.concatenate(
                [gate_grad.reshape(n, 1, UNIT, TILE), up_grad.reshape(n, 1, UNIT, TILE)], 1
            ).reshape(n * 2 * UNIT, TILE)
            wide = mm(both_grad, rows(r.xs, t), NN).reshape(PACK, 2, 2, UNIT, z.d)
            down = mm(hidden, rows(r.ys, t), NN).reshape(PACK, 2, UNIT, z.d)
            if t == 0:
                r.acc[:, :, 0:2] = wide
                r.acc[:, :, 2] = down
            else:
                r.acc[:, :, 0:2] += wide
                r.acc[:, :, 2] += down
        for k in range(PACK):
            g = i * PACK + k
            r.gsum[g] = r.acc[k, c]
            r.pair_s[g] = r.acc[k, 1 - c].astype(BF)

    def combine(g):
        pair(g).wait_recv()
        r.gsum[g] += r.pair_r[g].astype(F32)

    def add_chain(g):
        chain(g).wait_recv()
        r.gsum[g] += r.chain_r[g].astype(F32)

    def send_chain(g):
        r.chain_s[g] = r.gsum[g].astype(BF)
        chain(g).start()

    def split(unit):
        return unit.reshape(3, z.chips, z.rpo, z.d)

    def reduce_first(i):
        for k in range(PACK):
            g = i * PACK + k
            combine(g)

            @pl.when(p > 0)
            def _():
                add_chain(g)

            send_chain(g)

    def make_middle(g):
        combine(g)
        add_chain(g)
        middle = renormalize(r.wf[g, c].reshape(3, UNIT, z.d), r.gsum[g])
        r.midb[g] = middle.astype(BF)
        mid_out(g).start()

        @pl.when(g < z.nb)
        def _():
            pieces = split(middle)
            for t in range(z.chips):
                r.midq[g, t] = pieces[:, t].astype(BF)
                if t < z.chips - 1:
                    own_mid(g, t).start()

    def relay(g):
        mid_on(g).wait_recv()

        @pl.when(p < z.chips - 1)
        def _():
            mid_on(g).start()

        mid_part(g, c).start()

    def reduce_second(i):
        for k in range(PACK):
            g = i * PACK + k
            combine(g)

            @pl.when(both(g < z.nb, tail_chip))
            def _():
                send_chain(g)

            @pl.when(g >= z.nb)
            def _():
                pieces = split(r.gsum[g])
                for t in range(z.chips):
                    @pl.when(p != t)
                    def _():
                        r.ox_s[g - z.nb, t] = pieces[:, t].astype(BF)

                    @pl.when(p > t)
                    def _():
                        cross_grad(g - z.nb, t, p).start()

    def hand_back(i):
        for k in range(PACK):
            g = i * PACK + k

            @pl.when(g < z.nb)
            def _():
                add_chain(g)

                @pl.when(p > 0)
                def _():
                    send_chain(g)

                @pl.when(head_chip)
                def _():
                    pieces = split(r.gsum[g])
                    for t in range(z.chips):
                        r.og_s[g, t] = pieces[:, t].astype(BF)
                        own_grad(g, t).start()

    tile = WINDOW // 2

    def attention_tiles(h, tiles, bias):
        columns = pl.ds(pl.multiple_of(h * AH, AH), AH)

        def block(ref, halo_ref, at):
            if at < 0:
                return halo_ref[(at + 2) * tile : (at + 3) * tile, columns]
            return ref[at * tile : (at + 1) * tile, columns]

        def scores(t):
            keys = [block(r.ks, r.hk, t - 2 + n) for n in range(3)]
            biases = [bias if t - 2 + n < 0 else None for n in range(2)]
            return attend_scores(r.qs[t * tile : (t + 1) * tile, columns], keys, biases)

        ahead = scores(tiles[0])
        for n, t in enumerate(tiles):
            now = ahead
            if n + 1 < len(tiles):
                ahead = scores(tiles[n + 1])
            values = [block(r.vs, r.hv, t - 2 + m) for m in range(3)]
            r.att[t * tile : (t + 1) * tile, columns] = attend_values(*now, values)

    def hidden_step(i):
        n = PACK * 2 * UNIT
        w = weights(i)
        w_gu = jnp.concatenate([w[:, 0].reshape(n, z.d), w[:, 1].reshape(n, z.d)], 0)
        columns = pl.ds(pl.multiple_of(i * n, n), n)
        tiles = z.rows // SMALL

        def products(t):
            return mm(r.fqs[t * SMALL : (t + 1) * SMALL, :], w_gu, NT)

        ahead = products(0)
        for t in range(tiles):
            now = ahead
            if t + 1 < tiles:
                ahead = products(t + 1)
            gate, up = now[:, :n], now[:, n:]
            r.hid[t * SMALL : (t + 1) * SMALL, columns] = (gate * sigmoid(gate) * up).astype(BF)

    waits = either(first, s == z.half)

    def halo_tiles():
        @pl.when(s > 0)
        def _():
            with scope("halow"):
                for n in range(4):
                    halo(n).wait_recv()

        bias = jnp.where(s == 0, jnp.float32(NEG), jnp.float32(0.0))

        @pl.loop(0, z.heads)
        def _(h):
            with scope("atth"):
                attention_tiles(h, range(2), bias)

    @pl.loop(0, 2 * z.ns)
    def _(j):
        early, late = j < z.ns, j >= z.ns
        i = lax.rem(j, z.ns)

        @pl.when(either(both(first, j == 0), both(second, j == z.ns)))
        def _():
            load(4).wait()
            for n in range(2):
                load_rows(n, 0).wait()

        @pl.when(either(both(second, j == 0), both(first, j == z.ns)))
        def _():
            for n in (0, 1, 2):
                load(n).wait()

        @pl.when(j == z.ns)
        def _():
            load(3).wait()

        @pl.when(both(second, j == 0))
        def _():
            with scope("enter"):
                enter()

        @pl.when(both(first, early))
        def _():
            step = r.wf.at[pl.ds(i * PACK, PACK)]
            pltpu.make_async_copy(step, step, r.wf_sem.at[i]).wait()
            for k in range(PACK):
                g = i * PACK + k
                for core in range(2):
                    r.wb[g, core] = r.wf[g, core].reshape(3, UNIT, z.d).astype(BF)

            @pl.when(j == 0)
            def _():
                load_weights(PACK, z.ng)

        @pl.when(j == 1)
        def _():
            load_rest()

        differentiate = first == early

        def relay_next(k, ready):
            @pl.when(both(second, late, j < 2 * z.ns - 1, ready))
            def _():
                with scope("relay%d" % k):
                    relay((i + 1) * PACK + k)

        def between():
            @pl.when(either(both(first, j == 0), both(second, j == z.ns)))
            def _():
                for n in range(2):
                    load_rows(n, 1).wait()

            @pl.when(both(first, j == 0))
            def _():
                with scope("enter"):
                    enter()

            relay_next(0, i > 0)

            @pl.when(both(second, p < z.chips - 1, j >= z.ns + 3))
            def _():
                with scope("handback"):
                    hand_back(j - z.ns - 3)

            @pl.when(both(first, tail_chip, either(j == z.ns - 2, j == z.ns - 1)))
            def _():
                with scope("middle"):
                    make_middle(j - 1)

        def send_forward(low, high):
            @pl.when(both(second, j == 2 * z.ns - 1))
            def _():
                for t in range(1, z.chips):
                    @pl.when(p < t)
                    def _():
                        @pl.loop(low, high)
                        def _(g):
                            cross_grad(g, t, p).start()

        @pl.when(differentiate)
        def _():
            with scope("grad"):
                grad_step(i, between)

        @pl.when(jnp.logical_not(differentiate))
        def _():
            with scope("att"):
                attention_tiles(i, range(2, z.rows // tile), None)

        @pl.when(differentiate)
        def _():
            for k in range(PACK):
                pair(i * PACK + k).start()

        @pl.when(both(first, p < z.chips - 1, early))
        def _():
            with scope("rfirst"):
                reduce_first(i)

        relay_next(0, i == 0)
        relay_next(1, either(i >= z.ns - 3, both(tail_chip, i > 0)))

        start_halo(both(beside, j == z.ns + 1), range(4))
        start_halo(both(slow, j == z.ns + 2), (0, 2, 3))
        @pl.when(both(second, p < z.chips - 1, j == 2 * z.ns - 1))
        def _():
            with scope("handback"):
                hand_back(z.ns - 3)

        send_forward(0, z.nb - PACK)

        @pl.when(both(first, tail_chip, j > z.ns, j < 2 * z.ns - 1))
        def _():
            with scope("middle"):
                make_middle(j)

        @pl.when(late)
        def _():
            with scope("hidden"):
                hidden_step(i)

        relay_next(1, both(i < z.ns - 3, either(i == 0, p < z.chips - 1)))

        @pl.when(both(first, tail_chip, either(j == 1, j == 2, j == z.ns - 1, j == z.ns, j == 2 * z.ns - 2)))
        def _():
            with scope("middle"):
                make_middle(jnp.where(j < 3, j - 1, jnp.where(late, j + j // (2 * z.ns - 2), j)))

        @pl.when(both(second, late))
        def _():
            with scope("rsecond"):
                reduce_second(i)

        send_forward(z.nb - PACK, z.nb)

        start_halo(both(border, j == 2 * z.ns - 1), (2, 3))

        @pl.when(both(jnp.logical_not(waits), j == z.ns - 1))
        def _():
            halo_tiles()

        @pl.when(both(second, j >= z.ns - 1, j < 2 * z.ns - 1))
        def _():
            base = (j + 1 - z.ns) * PACK

            @pl.when(j == z.ns - 1)
            def _():
                for k in range(PACK):
                    relay(base + k)

            with scope("partw"):
                for k in range(PACK):
                    mid_part(base + k, 1 - c).wait_recv()

    w_down = r.wb[:, :, 2].reshape(z.ng * 2 * UNIT, z.d)

    def finish(low, high):
        spots = [pl.ds(n, SMALL) for n in range(low, high, SMALL)]
        with scope("down"):
            outs = [mm(r.hid[at, :], w_down, NN) for at in spots]
            for at, out in zip(spots, outs):
                inverse = lax.rsqrt(jnp.mean(out * out, axis=-1, keepdims=True) + EPSILON)
                r.outs[at, :] = (r.att[at, :] + out * inverse * r.gains[...]).astype(BF)
        at = pl.ds(low, high - low)
        pltpu.make_async_copy(r.outs.at[at], r.mixed.at[at], r.store_sem.at[0]).start()

    finish(WINDOW, z.rows)

    @pl.when(waits)
    def _():
        halo_tiles()

    finish(0, WINDOW)

    with scope("tailfin"):
        @pl.when(first)
        def _():
            @pl.loop(0, z.nb)
            def _(g):
                @pl.when(tail_chip)
                def _():
                    r.ownm[g] = r.midq[g, z.chips - 1]

                @pl.when(jnp.logical_not(tail_chip))
                def _():
                    with scope("ownmw"):
                        own_mid(g, 0).wait_recv()

                with scope("owngw"):
                    own_grad(g, 0).wait_recv()
                with scope("fin"):
                    r.rows_out[g] = renormalize(r.ownm[g].astype(F32), r.og_r[g].astype(F32))
                    pltpu.make_async_copy(r.rows_out.at[g], r.final.at[:, g], r.rows_sem.at[0]).start()

        @pl.when(second)
        def _():
            @pl.loop(0, z.nb)
            def _(g):
                total, middle = split(r.gsum[g + z.nb]), split(r.wb[g + z.nb, c].astype(F32))
                mine, base = total[:, 0], middle[:, 0]
                for t in range(1, z.chips):
                    mine = jnp.where(p == t, total[:, t], mine)
                    base = jnp.where(p == t, middle[:, t], base)
                for t in range(z.chips):
                    @pl.when(p != t)
                    def _():
                        with scope("crossw"):
                            cross_grad(g, t, t).wait_recv()
                for t in range(z.chips):
                    mine = mine + jnp.where(p == t, 0.0, r.ox_r[g, t].astype(F32))
                with scope("fin"):
                    r.rows_out[g] = renormalize(base, mine)
                    pltpu.make_async_copy(r.rows_out.at[g], r.final.at[:, g], r.rows_sem.at[0]).start()

    with scope("tailsend"):
        @pl.when(s < z.count - 1)
        def _():
            for n in range(4):
                halo(n).wait_send()

        def sent(ref, sem):
            remote(ref, ref, sem.at[0], sem.at[0], s).wait_send()

        sent(r.pair_s, r.pair_ss)

        @pl.when(both(first, p < z.chips - 1))
        def _():
            sent(r.chain_s, r.chain_ss)

        @pl.when(both(second, p > 0))
        def _():
            sent(r.chain_s.at[pl.ds(0, z.nb)], r.chain_ss)

        @pl.when(either(both(first, tail_chip), both(second, p < z.chips - 1)))
        def _():
            sent(r.midb, r.mid_ss)

        @pl.when(second)
        def _():
            sent(r.midb, r.part_ss)
            sent(r.ox_s.at[:, pl.ds(0, z.chips - 1)], r.ox_ss)

        @pl.when(both(first, tail_chip))
        def _():
            sent(r.midq.at[:, pl.ds(0, z.chips - 1)], r.om_ss)

        @pl.when(both(second, head_chip))
        def _():
            sent(r.og_s, r.og_ss)

    with scope("tailstore"):
        pltpu.make_async_copy(r.outs, r.mixed, r.store_sem.at[0]).wait()
        pltpu.make_async_copy(r.rows_out, r.rows_out, r.rows_sem.at[0]).wait()


def hand_over_kernel(m_ref, f_ref, mo_ref, fo_ref, m_buf, f_buf, m_in, m_out, f_sem):
    step = m_buf.shape[0] // PIECES
    pieces = [pl.ds(n * step, step) for n in range(PIECES)]
    fetches = [pltpu.make_async_copy(m_ref.at[at], m_buf.at[at], m_in.at[n]) for n, at in enumerate(pieces)]
    stores = [pltpu.make_async_copy(m_buf.at[at], mo_ref.at[at], m_out.at[n]) for n, at in enumerate(pieces)]
    f_fetch = pltpu.make_async_copy(f_ref, f_buf, f_sem.at[0])
    f_store = pltpu.make_async_copy(f_buf, fo_ref, f_sem.at[1])
    f_fetch.start()
    for fetch in fetches:
        fetch.start()
    f_fetch.wait()
    f_store.start()
    for fetch, store in zip(fetches, stores):
        fetch.wait()
        store.start()
    f_store.wait()
    for store in stores:
        store.wait()


def hand_over(mixed, final):
    hbm = pl.BlockSpec(memory_space=pltpu.HBM)
    dma = pltpu.SemaphoreType.DMA
    return pl.pallas_call(
        hand_over_kernel,
        out_shape=tuple(jax.ShapeDtypeStruct(a.shape, a.dtype) for a in (mixed, final)),
        in_specs=[hbm] * 2,
        out_specs=(hbm,) * 2,
        scratch_shapes=[
            pltpu.VMEM(mixed.shape, mixed.dtype), pltpu.VMEM(final.shape, final.dtype),
            dma((PIECES,)), dma((PIECES,)), dma((2,)),
        ],
        compiler_params=pltpu.CompilerParams(vmem_limit_bytes=LIMIT),
    )(mixed, final)


def shards(
    attn_query, attn_key, attn_value, fast_query, fast_key, fast_value, rates, fast_weights, gain
):
    rows, d = fast_key.shape
    f = fast_weights.shape[1]
    z = sizes(lax.axis_size("seq"), rows, d, f, attn_query.shape[1])
    weights = jnp.swapaxes(fast_weights[0], 0, 1).reshape(3, 2, z.chips, 2, z.nb, z.rpo, d)
    parts = scratch(z)
    anywhere = pl.BlockSpec(memory_space=pl.ANY)
    hbm = pl.BlockSpec(memory_space=pltpu.HBM)
    vmem = pl.BlockSpec(memory_space=pltpu.VMEM)
    mixed, final = pl.pallas_call(
        functools.partial(kernel, z, INPUTS + ("mixed", "final") + tuple(parts)),
        out_shape=(
            jax.ShapeDtypeStruct((rows, d), BF),
            jax.ShapeDtypeStruct((3, z.nb, z.rpo, d), F32),
        ),
        in_specs=[hbm] * 9,
        out_specs=(anywhere, anywhere),
        scratch_shapes=list(parts.values()),
        compiler_params=pltpu.CompilerParams(
            vmem_limit_bytes=LIMIT, collective_id=0, has_side_effects=True
        ),
    )(
        attn_query, attn_key, attn_value, fast_query, fast_key, fast_value,
        rates.reshape(1, rows), weights, gain,
    )
    mixed, final = hand_over(mixed, final)
    return (mixed, jnp.swapaxes(final.reshape(3, z.share, d), 0, 1)[None])


def solution(mesh):
    tokens = P("seq", "head")
    in_specs = (tokens,) * 7 + (P("head", None, None, None), P("head", None))
    out_specs = (tokens, P("head", "seq", None, None))
    return jax.shard_map(shards, mesh=mesh, in_specs=in_specs, out_specs=out_specs, check_vma=False)
```
